256 devices in a mesh: pts: 32 (over y, z), own: 8 (over x, core).
Axes of the slice: x: 4, y: 4, z: 8, core: 2. Of those that a mesh axis runs over, the one named last changes fastest.
Arguments:
- points: bfloat16 [65536, 1536], P(('pts', 'own')), may hold values from -6 to 6
- parent_of: int32 [65536, 1], P('pts'), may hold values from 0 to 127, as said below
- owner_of: int32 [128], replicated, may hold values from 0 to 7, as said below
- child_count: int32 [128], replicated, may hold values from 16 to 64, as said below
- centroids: bfloat16 [8, 1024, 1536], P('own'), may hold values from -6 to 6
Outputs:
- new_centroids: bfloat16 [8, 1024, 1536], P('own', 'pts')
The draws below stay inside these ranges and needn't reach their ends.
Inputs may be any that keep to these rules, and one draw needn't show every extreme that they name: `owner_of`: each owner is named by exactly 16 parents. `child_count`: exactly 64 for at least one parent. `parent_of`: every parent is named by some point; in the 256 rows of one device, exactly 64 rows have parents of one owner, and all devices with the same pts index pick the same such owner; the rest of the device's rows go to the other owners as evenly as possible, so no owner gets more than 64 rows of one device.
All inputs are finite; a program needn't handle non-finite values.
Results may differ from the reference program's by a relative error of at most 0.0031.
Values may be sent and summed in bfloat16 or wider, within the bound.
A program may use at most 128 MiB of HBM per device.

```python
import jax
import jax.numpy as jnp
from jax import lax

D = 1536
MC = 64
GO = 16
SWEEPS = 2
TOK_DEV = 256
KO = 1024
G = 128
POINTS = 65536


def parent_order(key):
    return jax.random.permutation(jax.random.fold_in(key, 11), G).astype(jnp.int32)


def draw_owner_of(key, part):
    order = parent_order(key)
    ranks = jnp.arange(G, dtype=jnp.int32) // GO
    return jnp.zeros((G,), jnp.int32).at[order].set(ranks)


def draw_child_count(key, part):
    counts = jax.random.randint(jax.random.fold_in(key, 23), (G,), MC // 4, MC + 1)
    where_full = jax.random.randint(jax.random.fold_in(key, 37), (), 0, G)
    return counts.at[where_full].set(MC).astype(jnp.int32)


def draw_parent_of(key, part):
    order = parent_order(key)
    owners = G // GO
    blocks = POINTS // TOK_DEV
    cap = 2 * TOK_DEV // owners
    shift = jax.random.randint(jax.random.fold_in(key, 41), (), 0, owners)
    block_ids = jnp.arange(blocks, dtype=jnp.int32)
    full_owner = (block_ids // owners + shift) % owners
    offsets = jax.random.randint(jax.random.fold_in(key, 43), (blocks,), 0, owners - 1)
    noise = jax.random.randint(jax.random.fold_in(key, 47), (blocks, TOK_DEV), 0, 1 << 20)
    scores = noise * TOK_DEV + jnp.arange(TOK_DEV, dtype=jnp.int32)[None, :]
    placed = jnp.argsort(scores, axis=1)
    rank = jnp.argsort(placed, axis=1).astype(jnp.int32)
    rest = rank - cap
    other = (full_owner[:, None] + 1 + (rest + offsets[:, None]) % (owners - 1)) % owners
    owner = jnp.where(rank < cap, full_owner[:, None], other)
    loose = jax.random.randint(jax.random.fold_in(key, 53), (blocks, TOK_DEV), 0, GO)
    within = jnp.where(rank < cap, rank % GO, loose)
    parent = order[(owner * GO + within).reshape(-1)]
    return parent.reshape(POINTS, 1).astype(jnp.int32)


def centroid_table(key):
    owners = G // GO
    sub = jax.random.fold_in(key, 61)
    values = jax.random.normal(sub, (owners, KO, D), jnp.float32)
    return jnp.clip(values, -6.0, 6.0)


def draw_centroids(key, part):
    return centroid_table(key).astype(jnp.bfloat16)


def draw_points(key, part):
    parent = draw_parent_of(key, part)[:, 0]
    owners_of = draw_owner_of(key, part)
    counts = draw_child_count(key, part)
    parent_range = jnp.arange(G, dtype=jnp.int32)
    same_owner = owners_of[:, None] == owners_of[None, :]
    earlier = parent_range[None, :] < parent_range[:, None]
    first = jnp.sum(jnp.where(same_owner & earlier, counts[None, :], 0), axis=1).astype(jnp.int32)
    row_owner = owners_of[parent]
    row_first = first[parent]
    row_count = counts[parent]
    pick_one = jax.random.randint(jax.random.fold_in(key, 71), (POINTS,), 0, row_count)
    pick_two = jax.random.randint(jax.random.fold_in(key, 73), (POINTS,), 0, row_count)
    primary = jnp.minimum(pick_one, pick_two)
    step_over = jax.random.randint(jax.random.fold_in(key, 79), (POINTS,), 0, row_count - 1)
    second = (primary + 1 + step_over) % row_count
    table = centroid_table(key).reshape(-1, D)
    base_row = row_owner * KO + row_first
    near = table[base_row + primary]
    beside = table[base_row + second]
    lead = jax.random.uniform(jax.random.fold_in(key, 83), (POINTS, 1), jnp.float32, 0.5, 0.8)
    trail = jax.random.uniform(jax.random.fold_in(key, 89), (POINTS, 1), jnp.float32, 0.3, 0.6)
    noise = jax.random.normal(jax.random.fold_in(key, 97), (POINTS, D), jnp.float32)
    values = lead * near + trail * beside + noise
    return jnp.clip(values, -6.0, 6.0).astype(jnp.bfloat16)


def setup_inputs(seed: int = 0) -> dict:
    splits = jax.random.split(jax.random.key(seed), 6)
    return {
        "points": draw_points(jax.random.fold_in(splits[5], 71), 0),
        "parent_of": draw_parent_of(jax.random.fold_in(splits[5], 71), 0),
        "owner_of": draw_owner_of(jax.random.fold_in(splits[5], 71), 0),
        "child_count": draw_child_count(jax.random.fold_in(splits[5], 71), 0),
        "centroids": draw_centroids(jax.random.fold_in(splits[5], 71), 0),
    }


def unit_rms(values):
    values = values.astype(jnp.float32)
    return values * lax.rsqrt(lax.optimization_barrier(jnp.mean(values * values, axis=-1, keepdims=True)) + 1e-06)

def reference(points, parent_of, owner_of, child_count, centroids):
    width = points.shape[1]
    point_unit = unit_rms(points).astype(jnp.bfloat16)
    parent_ids = parent_of[:, 0]
    parent_range = jnp.arange(owner_of.shape[0], dtype=jnp.int32)
    same_owner = owner_of[:, None] == owner_of[None, :]
    earlier = parent_range[None, :] < parent_range[:, None]
    first_slot = lax.optimization_barrier(jnp.sum(jnp.where(same_owner & earlier, child_count[None, :], 0), axis=1)).astype(jnp.int32)
    row_owner = owner_of[parent_ids]
    row_first = first_slot[parent_ids]
    row_count = child_count[parent_ids]
    slot_index = jnp.arange(KO, dtype=jnp.int32)

    def per_owner(owner):
        cent_unit = unit_rms(centroids[owner]).astype(jnp.bfloat16)
        in_range = (row_owner == owner)[:, None] & (slot_index[None, :] >= row_first[:, None]) & (slot_index[None, :] < (row_first + row_count)[:, None])
        table_range = (owner_of == owner)[:, None] & (slot_index[None, :] >= first_slot[:, None]) & (slot_index[None, :] < (first_slot + child_count)[:, None])
        slot_used = jnp.any(table_range, axis=0)
        row_live = row_owner == owner
        scores = jnp.dot(point_unit, cent_unit.T, preferred_element_type=jnp.float32) / (width * 0.05)
        weights = jnp.where(in_range, jnp.exp(scores), jnp.float32(0.0))
        for sweep in range(SWEEPS):
            column_sum = lax.optimization_barrier(jnp.sum(weights, axis=0))
            weights = weights / jnp.where(slot_used, column_sum, jnp.float32(1.0))[None, :]
            row_sum = lax.optimization_barrier(jnp.sum(weights, axis=1))
            weights = weights / jnp.where(row_live, row_sum, jnp.float32(1.0))[:, None]
        assign = weights.astype(jnp.bfloat16)
        moved = jnp.dot(assign.T, point_unit, preferred_element_type=jnp.float32)
        return unit_rms(cent_unit.astype(jnp.float32) + 8.0 * moved).astype(jnp.bfloat16)
    return lax.map(per_owner, jnp.arange(centroids.shape[0], dtype=jnp.int32))
```

```python
import functools

import jax
import jax.numpy as jnp
from jax import lax
from jax.experimental import pallas as pl
from jax.experimental.pallas import tpu as pltpu
from jax.sharding import PartitionSpec as P

SWEEPS = 2
CAP = 64
CORES = 2
NY = 4
MESH = pl.DeviceIdType.MESH
F32 = jnp.float32
BF16 = jnp.bfloat16

TILES = (
    ("yz", 0, 256, 1),
    ("zy", 1024, 256, 1),
    ("yz", 256, 256, -1),
    ("yz", 512, 256, 1),
    ("zy", 1280, 256, -1),
    ("yz", 768, 256, -1),
)


def unit_rms(values):
    values = values.astype(F32)
    return values * lax.rsqrt(jnp.mean(values * values, axis=-1, keepdims=True) + 1e-06)


def iota(shape, dim):
    return lax.broadcasted_iota(jnp.int32, shape, dim).astype(F32)


def kernel(
    ny, nz, nx,
    points_ref, parent_ref, owner_ref, count_ref, cent_hbm, out_ref,
    cent_raw, cent_unit, point_unit, packed, rows, member, onehot, place, weights, assign_t, part, final,
    ysum_send, ysum_recv, zsum_send, zsum_recv, tile_bufs,
    cent_sem, x_send, x_recv, ys_send, ys_recv, zs_send, zs_recv, rs_send, rs_recv,
):
    pts, me = lax.axis_index("pts"), lax.axis_index("own")
    y, z = lax.div(pts, nz), lax.rem(pts, nz)
    x, core = lax.div(me, CORES), lax.rem(me, CORES)
    groups = nx * CORES
    width = points_ref.shape[1]
    tokens = points_ref.shape[0]
    parents = owner_ref.shape[1]
    slots = cent_hbm.shape[0]

    def own_at(dx, dc, sign):
        other = lax.rem(x + (dx if sign > 0 else nx - dx), nx)
        return other * CORES + (core if dc == 0 else 1 - core)

    def at_y(step):
        return lax.rem(y + step + ny, ny)

    def at_z(step):
        return lax.rem(z + step + nz, nz)

    def dev_y(step):
        return (at_y(step) * nz + z, me)

    def dev_z(step):
        return (y * nz + at_z(step), me)

    offsets = [(dx, dc) for dx in range(nx) for dc in range(CORES)]
    barrier = pltpu.get_barrier_semaphore()
    peers = [(pts, own_at(dx, dc, 1)) for dx, dc in offsets if (dx, dc) != (0, 0)]
    peers += [dev_y(s) for s in range(1, ny)] + [dev_z(s) for s in range(1, nz)]
    for peer in peers:
        pl.semaphore_signal(barrier, inc=1, device_id=peer, device_id_type=MESH)
    cent_copy = pltpu.make_async_copy(cent_hbm, cent_raw, cent_sem)
    cent_copy.start()

    pending = []

    def send(src, dst, send_sem, recv_sem, device):
        copy = pltpu.make_async_remote_copy(
            src_ref=src, dst_ref=dst, send_sem=send_sem, recv_sem=recv_sem,
            device_id=device, device_id_type=MESH,
        )
        copy.start()
        pending.append(copy)
        return copy

    square = (parents, parents)
    owner_row = owner_ref[...].astype(F32)
    count_row = count_ref[...].astype(F32)
    diagonal = iota(square, 0) == iota(square, 1)
    owner_col = jnp.sum(jnp.where(diagonal, owner_row, 0.0), axis=1, keepdims=True)
    count_col = jnp.sum(jnp.where(diagonal, count_row, 0.0), axis=1, keepdims=True)
    upper = jnp.where(iota((tokens, tokens), 0) <= iota((tokens, tokens), 1), 1.0, 0.0).astype(BF16)
    parent_iota = iota((parents, tokens), 0)

    def owners_of_block(index):
        parent = parent_ref[pl.ds(index, 1), :].astype(F32)
        return parent, jnp.sum(jnp.where(parent_iota == parent, owner_col, 0.0), axis=0, keepdims=True)

    _, my_owner = owners_of_block(me)
    goes = my_owner == iota((groups, tokens), 0)
    rank = jnp.dot(jnp.where(goes, 1.0, 0.0).astype(BF16), upper, preferred_element_type=F32)
    place[...] = jnp.where(goes, rank - 1.0, -1.0)
    point_unit[...] = unit_rms(points_ref[...]).astype(BF16)

    slot_iota = iota((CAP, tokens), 0)

    def pack(group):
        picks = [
            jnp.where(place[pl.ds(own_at(dx, dc, 1), 1), :] == slot_iota, 1.0, 0.0).astype(BF16) for dx, dc in group
        ]
        return jnp.dot(jnp.concatenate(picks, axis=0), point_unit[...], preferred_element_type=F32).astype(BF16)

    far = [(dx, dc) for dx in range(nx // 2, nx // 2 + 1) for dc in range(CORES)]
    near = [(dx, dc) for dx in (1, nx - 1) for dc in range(CORES)]
    here = [(0, 1), (0, 0)]
    block_of = {offset: i for i, offset in enumerate(here + near + far)}
    arrivals = {}
    waited = False
    for group in (far, near, here):
        block = pack(group)
        for i, (dx, dc) in enumerate(group):
            k = block_of[dx, dc]
            value = block[i * CAP:(i + 1) * CAP]
            if (dx, dc) == (0, 0):
                rows[pl.ds(k * CAP, CAP), :] = value
            else:
                packed[pl.ds(k * CAP, CAP), :] = value
        if not waited:
            pl.semaphore_wait(barrier, len(peers))
            waited = True
        for dx, dc in group:
            k = block_of[dx, dc]
            if (dx, dc) != (0, 0):
                span = pl.ds(k * CAP, CAP)
                arrivals[k] = send(
                    packed.at[span], rows.at[span], x_send.at[k], x_recv.at[k], (pts, own_at(dx, dc, 1))
                )

    first_col = jnp.sum(
        jnp.where((owner_col == owner_row) & (iota(square, 1) < iota(square, 0)), count_row, 0.0),
        axis=1, keepdims=True,
    )
    my_index = me.astype(F32)
    slot_row = iota((parents, slots), 1)
    member[...] = jnp.where(
        (owner_col == my_index) & (slot_row >= first_col) & (slot_row < first_col + count_col), 1.0, 0.0
    ).astype(BF16)
    block_parent, block_live = [], []
    for dx, dc in here + near + far:
        parent, owner = owners_of_block(own_at(dx, dc, -1))
        block_parent.append(parent)
        block_live.append(owner == my_index)
    live = jnp.concatenate([jnp.where(one, 1.0, 0.0) for one in block_live], axis=0)
    rank = jnp.dot(live.astype(BF16), upper, preferred_element_type=F32)
    spot = jnp.where(live > 0.5, rank - 1.0, -1.0)
    for k in range(groups):
        chosen = spot[k:k + 1, :] == slot_iota
        parent = jnp.sum(jnp.where(chosen, block_parent[k] + 1.0, 0.0), axis=1, keepdims=True) - 1.0
        onehot[k * CAP:(k + 1) * CAP, :] = jnp.where(parent == iota((CAP, parents), 1), 1.0, 0.0).astype(BF16)

    cent_copy.wait()
    step_rows = 64

    @pl.loop(0, slots // step_rows)
    def _(i):
        span = pl.ds(pl.multiple_of(i * step_rows, step_rows), step_rows)
        cent_unit[span, :] = unit_rms(cent_raw[span, :]).astype(BF16)

    half = groups // 2
    tall = half * CAP
    scale = 1.0 / (width * 0.05)
    wide = 256
    sums = [None] * (slots // wide)
    for h in range(2):
        for k in range(h * half, (h + 1) * half):
            if k in arrivals:
                arrivals[k].wait_recv()
        span = slice(h * tall, (h + 1) * tall)
        for n in range(slots // wide):
            cols = slice(n * wide, (n + 1) * wide)
            score = lax.dot_general(
                rows[span, :], cent_unit[cols, :], (((1,), (1,)), ((), ())), preferred_element_type=F32
            )
            allowed = jnp.dot(onehot[span, :], member[:, cols], preferred_element_type=F32)
            value = jnp.where(allowed > 0.5, jnp.exp(score * scale), 0.0)
            weights[span, cols] = value
            total = jnp.sum(value, axis=0, keepdims=True)
            sums[n] = total if h == 0 else sums[n] + total
    column = jnp.concatenate(sums, axis=1)

    def column_total(sweep, local):
        ysum_send[sweep] = local
        copies = [
            send(ysum_send.at[sweep], ysum_recv.at[sweep, s - 1], ys_send.at[sweep, s - 1],
                 ys_recv.at[sweep, s - 1], dev_y(s))
            for s in range(1, ny)
        ]
        total = local
        for s, copy in enumerate(copies):
            copy.wait_recv()
            total = total + ysum_recv[sweep, s]
        zsum_send[sweep] = total
        copies = [
            send(zsum_send.at[sweep], zsum_recv.at[sweep, s - 1], zs_send.at[sweep, s - 1],
                 zs_recv.at[sweep, s - 1], dev_z(s))
            for s in range(1, nz)
        ]
        for s, copy in enumerate(copies):
            copy.wait_recv()
            total = total + zsum_recv[sweep, s]
        return total

    row_step = 128
    for sweep in range(SWEEPS):
        total = column_total(sweep, column)
        inverse = 1.0 / jnp.where(total > 0.0, total, 1.0)
        column = None
        for i in range(groups * CAP // row_step):
            span = slice(i * row_step, (i + 1) * row_step)
            value = weights[span, :] * inverse
            row_sum = jnp.sum(value, axis=1, keepdims=True)
            value = value * (1.0 / jnp.where(row_sum > 0.0, row_sum, 1.0))
            if sweep < SWEEPS - 1:
                weights[span, :] = value
                partial = jnp.sum(value, axis=0, keepdims=True)
                column = partial if column is None else column + partial
            else:
                assign_t[:, span] = jnp.transpose(value).astype(BF16)

    share = slots // (ny * nz)
    sem_base = 0
    tasks = []
    buf_at = 0
    for index, (order, first, cols, long) in enumerate(TILES):
        counts = [(ny if a == "y" else nz) - 1 for a in order]
        bufs = tile_bufs[buf_at:buf_at + 5]
        buf_at += 5
        tasks.append((index, order, first, cols, long, sem_base, bufs))
        sem_base += sum(counts)

    def run_tile(order, first, cols, long, base, bufs):
        send1, recv1, middle, send2, recv2 = bufs
        window = pl.ds(first, cols)

        def ring(axis, own_chunk, send_buf, recv_buf, sems):
            n = ny if axis == "y" else nz
            at, dev = (at_y, dev_y) if axis == "y" else (at_z, dev_z)
            far_steps, near_steps = n // 2, n // 2 - 1
            got = {}
            for t in range(1, far_steps + 1):
                for name, direction, steps, offset in (
                    ("far", long, far_steps, 0), ("near", -long, near_steps, far_steps)
                ):
                    if t > steps:
                        continue
                    slot = offset + t - 1
                    value = own_chunk(at(direction * (steps - t + 1)))
                    if t > 1:
                        got[name].wait_recv()
                        value = value + recv_buf[slot - 1].astype(F32)
                    send_buf[slot] = value.astype(BF16)
                    got[name] = send(
                        send_buf.at[slot], recv_buf.at[slot], rs_send.at[sems + slot], rs_recv.at[sems + slot],
                        dev(direction),
                    )
                yield
            value = own_chunk(at(0))
            for name, slot in (("far", far_steps - 1), ("near", n - 2)):
                if name in got:
                    got[name].wait_recv()
                    value = value + recv_buf[slot].astype(F32)
            result.append(value)

        product = jnp.dot(assign_t[...], rows[:, first:first + cols], preferred_element_type=F32)
        part[:, :, :, first:first + cols] = product.reshape(ny, nz, share, cols)
        result = []
        if order[0] == "y":
            yield from ring("y", lambda k: part[pl.ds(k, 1), :, :, window][0], send1, recv1, base)
        else:
            yield from ring("z", lambda k: part[:, pl.ds(k, 1), :, window][:, 0], send1, recv1, base)
        middle[...] = result.pop()
        base2 = base + (ny if order[0] == "y" else nz) - 1
        yield from ring(order[1], lambda k: middle[pl.ds(k, 1)][0], send2, recv2, base2)
        final[:, first:first + cols] = result.pop()

    running = []
    waiting = list(tasks)
    while running or waiting:
        if waiting:
            _, order, first, cols, long, base, bufs = waiting.pop(0)
            running.append(run_tile(order, first, cols, long, base, bufs))
        alive = []
        for one in running:
            try:
                next(one)
                alive.append(one)
            except StopIteration:
                pass
        running = alive

    base = cent_unit[pl.ds(pl.multiple_of(pts * share, share), share), :].astype(F32)
    out_ref[...] = unit_rms(base + 8.0 * final[...]).astype(BF16)
    for copy in pending:
        copy.wait_send()


def local(mesh_pts, mesh_own, points, parent_of, owner_of, child_count, centroids):
    ny = NY
    nz = mesh_pts // ny
    nx = mesh_own // CORES
    tokens, width = points.shape
    slots = centroids.shape[1]
    parents = owner_of.shape[0]
    share = slots // mesh_pts
    groups = mesh_own
    tile_shapes = []
    sems = 0
    for order, first, cols, long in TILES:
        n1, n2 = (ny, nz) if order == "yz" else (nz, ny)
        tile_shapes += [
            pltpu.VMEM((n1 - 1, n2, share, cols), BF16),
            pltpu.VMEM((n1 - 1, n2, share, cols), BF16),
            pltpu.VMEM((n2, share, cols), F32),
            pltpu.VMEM((n2 - 1, share, cols), BF16),
            pltpu.VMEM((n2 - 1, share, cols), BF16),
        ]
        sems += n1 + n2 - 2
    dma = pltpu.SemaphoreType.DMA
    out = pl.pallas_call(
        functools.partial(kernel_entry, ny, nz, nx, len(tile_shapes)),
        out_shape=jax.ShapeDtypeStruct((share, width), BF16),
        in_specs=[pl.BlockSpec(memory_space=pltpu.VMEM)] * 4 + [pl.BlockSpec(memory_space=pl.ANY)],
        out_specs=pl.BlockSpec(memory_space=pltpu.VMEM),
        scratch_shapes=[
            pltpu.VMEM((slots, width), BF16),
            pltpu.VMEM((slots, width), BF16),
            pltpu.VMEM((tokens, width), BF16),
            pltpu.VMEM((groups * CAP, width), BF16),
            pltpu.VMEM((groups * CAP, width), BF16),
            pltpu.VMEM((parents, slots), BF16),
            pltpu.VMEM((groups * CAP, parents), BF16),
            pltpu.VMEM((groups, tokens), F32),
            pltpu.VMEM((groups * CAP, slots), F32),
            pltpu.VMEM((slots, groups * CAP), BF16),
            pltpu.VMEM((ny, nz, share, width), F32),
            pltpu.VMEM((share, width), F32),
            pltpu.VMEM((SWEEPS, 1, slots), F32),
            pltpu.VMEM((SWEEPS, ny - 1, 1, slots), F32),
            pltpu.VMEM((SWEEPS, 1, slots), F32),
            pltpu.VMEM((SWEEPS, nz - 1, 1, slots), F32),
            *tile_shapes,
            dma,
            dma((groups,)),
            dma((groups,)),
            dma((SWEEPS, ny - 1)),
            dma((SWEEPS, ny - 1)),
            dma((SWEEPS, nz - 1)),
            dma((SWEEPS, nz - 1)),
            dma((sems,)),
            dma((sems,)),
        ],
        compiler_params=pltpu.CompilerParams(
            collective_id=0, has_side_effects=True, vmem_limit_bytes=60 * 1024 * 1024
        ),
    )(
        points,
        parent_of.reshape(groups, tokens),
        owner_of.reshape(1, parents),
        child_count.reshape(1, parents),
        centroids[0],
    )
    return out[None]


def kernel_entry(ny, nz, nx, tiles, *refs):
    head, rest = refs[:6 + 16], refs[6 + 16:]
    return kernel(ny, nz, nx, *head, rest[:tiles], *rest[tiles:])


def solution(mesh):
    in_specs = (P(("pts", "own"), None), P("pts", None), P(), P(), P("own", None, None))
    out_specs = P("own", "pts", None)
    body = functools.partial(local, mesh.shape["pts"], mesh.shape["own"])
    return jax.shard_map(body, mesh=mesh, in_specs=in_specs, out_specs=out_specs, check_vma=False)
```

```python
import functools

import jax
import jax.numpy as jnp
from jax import lax
from jax.experimental import pallas as pl
from jax.experimental.pallas import tpu as pltpu
from jax.sharding import PartitionSpec as P

SWEEPS = 2
CAP = 64
CORES = 2
NY = 4
MESH = pl.DeviceIdType.MESH
F32 = jnp.float32
BF16 = jnp.bfloat16

TILES = (
    ("yz", 256, -1, "direct"),
    ("zy", 128, 1, "ring"),
    ("yz", 128, 1, "ring"),
    ("yz", 256, 1, "direct"),
    ("zy", 128, -1, "direct"),
    ("zy", 128, 1, "direct"),
    ("zy", 128, 1, "direct"),
    ("zy", 128, -1, "ring"),
    ("zy", 128, -1, "direct"),
    ("yz", 128, -1, "ring"),
)


def stage_messages(mode, n, long):
    far = n // 2
    if mode == "ring":
        return [("far", t, long, 1) for t in range(1, far + 1)] + [("near", t, -long, 1) for t in range(1, far)]
    return [("one", long * far, long, far)] + [
        ("one", hops * way, way, hops) for hops in range(far - 1, 0, -1) for way in (long, -long)
    ]


def tile_tasks(index, tile, sizes, slots):
    order, cols, long, mode = tile
    share = slots
    for axis in order:
        share //= sizes[axis]
    tasks = {(index, "product"): ((), (), cols * 0.0027, ())}
    before = (index, "product")
    for stage, axis in enumerate(order):
        n = sizes[axis]
        chunk = (slots // n if stage == 0 else share) * cols
        work = chunk * 1.8e-6
        kind = "ring" if stage == 0 else mode
        messages = stage_messages(kind, n, long)
        names = [(index, stage, name, step) for name, step, _, _ in messages]
        wire = [(name, axis, way, hops, chunk * 2) for name, (_, _, way, hops) in zip(names, messages)]
        done = (index, stage, "sum")
        if kind == "ring":
            for key, one in zip(names, wire):
                last = key[:3] + (key[3] - 1,)
                first = key[3] == 1
                tasks[key] = ((before,) if first else (last,), () if first else (last,), work, (one,))
            ends = [(index, stage, "far", n // 2)] + ([(index, stage, "near", n // 2 - 1)] if n > 2 else [])
            tasks[done] = (tuple(ends), tuple(ends), 2 * work, ())
        else:
            tasks[index, stage, "all"] = ((before,), (), n * work, tuple(wire))
            tasks[done] = (((index, stage, "all"),), tuple(names), n * work, ())
        before = done
    return tasks


def schedule(sizes, slots):
    rate, hop_us, next_hop_us = 46500.0, 1.9, 0.75
    tasks = {}
    for index, tile in enumerate(TILES):
        tasks.update(tile_tasks(index, tile, sizes, slots))
    sender = {message[0]: key for key, task in tasks.items() for message in task[3]}
    after = {key: [] for key in tasks}
    for key, (before, waits, _, _) in tasks.items():
        for one in before:
            after[one].append((key, 0.0))
        for one in waits:
            after[sender[one]].append((key, hop_us))
    chain = {}

    def length(key):
        if key not in chain:
            chain[key] = tasks[key][2] + max([gap + length(one) for one, gap in after[key]], default=0.0)
        return chain[key]

    now, order, arrival, link_free, done = 0.0, [], {}, {}, set()
    while len(order) < len(tasks):
        ready = []
        for key, (before, waits, _, _) in tasks.items():
            if key not in done and all(one in done for one in before) and all(one in arrival for one in waits):
                ready.append((max([arrival[one] for one in waits], default=0.0), key))
        started = [one for one in ready if one[0] <= now]
        if started:
            at, key = max(started, key=lambda one: length(one[1]))
        else:
            at, key = min(ready, key=lambda one: (one[0], -length(one[1])))
        now = max(now, at) + tasks[key][2]
        for name, axis, way, hops, size in tasks[key][3]:
            start = max(now, link_free.get((axis, way), 0.0))
            link_free[axis, way] = start + hops * size / rate
            arrival[name] = link_free[axis, way] + hop_us + next_hop_us * (hops - 1)
        done.add(key)
        order.append(key)
    return order


def unit_rms(values):
    values = values.astype(F32)
    return values * lax.rsqrt(jnp.mean(values * values, axis=-1, keepdims=True) + 1e-06)


def iota(shape, dim):
    return lax.broadcasted_iota(jnp.int32, shape, dim).astype(F32)


def kernel(
    ny, nz, nx,
    points_ref, parent_ref, owner_ref, count_ref, cent_hbm, out_ref,
    cent_raw, cent_unit, point_unit, packed, rows, member, onehot, place, weights, assign_t, part, final,
    ysum_send, ysum_recv, zsum_send, zsum_recv, tile_bufs,
    cent_sem, x_send, x_recv, ys_send, ys_recv, zs_send, zs_recv, rs_send, rs_recv,
):
    pts, me = lax.axis_index("pts"), lax.axis_index("own")
    y, z = lax.div(pts, nz), lax.rem(pts, nz)
    x, core = lax.div(me, CORES), lax.rem(me, CORES)
    groups = nx * CORES
    width = points_ref.shape[1]
    tokens = points_ref.shape[0]
    parents = owner_ref.shape[1]
    slots = cent_hbm.shape[0]

    def own_at(dx, dc, sign):
        other = lax.rem(x + (dx if sign > 0 else nx - dx), nx)
        return other * CORES + (core if dc == 0 else 1 - core)

    def at_y(step):
        return lax.rem(y + step + ny, ny)

    def at_z(step):
        return lax.rem(z + step + nz, nz)

    def dev_y(step):
        return (at_y(step) * nz + z, me)

    def dev_z(step):
        return (y * nz + at_z(step), me)

    offsets = [(dx, dc) for dx in range(nx) for dc in range(CORES)]
    barrier = pltpu.get_barrier_semaphore()
    peers = [(pts, own_at(dx, dc, 1)) for dx, dc in offsets if (dx, dc) != (0, 0)]
    peers += [dev_y(s) for s in range(1, ny)] + [dev_z(s) for s in range(1, nz)]
    for peer in peers:
        pl.semaphore_signal(barrier, inc=1, device_id=peer, device_id_type=MESH)
    cent_copy = pltpu.make_async_copy(cent_hbm, cent_raw, cent_sem)
    cent_copy.start()

    pending = []

    def send(src, dst, send_sem, recv_sem, device):
        copy = pltpu.make_async_remote_copy(
            src_ref=src, dst_ref=dst, send_sem=send_sem, recv_sem=recv_sem,
            device_id=device, device_id_type=MESH,
        )
        copy.start()
        pending.append(copy)
        return copy

    square = (parents, parents)
    owner_row = owner_ref[...].astype(F32)
    count_row = count_ref[...].astype(F32)
    diagonal = iota(square, 0) == iota(square, 1)
    owner_col = jnp.sum(jnp.where(diagonal, owner_row, 0.0), axis=1, keepdims=True)
    count_col = jnp.sum(jnp.where(diagonal, count_row, 0.0), axis=1, keepdims=True)
    upper = jnp.where(iota((tokens, tokens), 0) <= iota((tokens, tokens), 1), 1.0, 0.0).astype(BF16)
    parent_iota = iota((parents, tokens), 0)

    def owners_of_block(index):
        parent = parent_ref[:, pl.ds(pl.multiple_of(index * tokens, tokens), tokens)].astype(F32)
        return parent, jnp.sum(jnp.where(parent_iota == parent, owner_col, 0.0), axis=0, keepdims=True)

    _, my_owner = owners_of_block(me)
    goes = my_owner == iota((groups, tokens), 0)
    rank = jnp.dot(jnp.where(goes, 1.0, 0.0).astype(BF16), upper, preferred_element_type=F32)
    place[...] = jnp.where(goes, rank - 1.0, -1.0)
    point_unit[...] = unit_rms(points_ref[...]).astype(BF16)

    slot_iota = iota((CAP, tokens), 0)

    def pack(group):
        picks = [
            jnp.where(place[pl.ds(own_at(dx, dc, 1), 1), :] == slot_iota, 1.0, 0.0).astype(BF16) for dx, dc in group
        ]
        return jnp.dot(jnp.concatenate(picks, axis=0), point_unit[...], preferred_element_type=F32).astype(BF16)

    far = [(dx, dc) for dx in range(nx // 2, nx // 2 + 1) for dc in range(CORES)]
    near = [(dx, dc) for dx in (1, nx - 1) for dc in range(CORES)]
    here = [(0, 1), (0, 0)]
    block_of = {offset: i for i, offset in enumerate(here + far + near)}
    arrivals = {}
    waited = False
    for group in (far, near, here):
        block = pack(group)
        for i, (dx, dc) in enumerate(group):
            k = block_of[dx, dc]
            value = block[i * CAP:(i + 1) * CAP]
            if (dx, dc) == (0, 0):
                rows[pl.ds(k * CAP, CAP), :] = value
            else:
                packed[pl.ds(k * CAP, CAP), :] = value
        if not waited:
            pl.semaphore_wait(barrier, len(peers))
            waited = True
        for dx, dc in group:
            k = block_of[dx, dc]
            if (dx, dc) != (0, 0):
                span = pl.ds(k * CAP, CAP)
                arrivals[k] = send(
                    packed.at[span], rows.at[span], x_send.at[k], x_recv.at[k], (pts, own_at(dx, dc, 1))
                )

    first_col = jnp.sum(
        jnp.where((owner_col == owner_row) & (iota(square, 1) < iota(square, 0)), count_row, 0.0),
        axis=1, keepdims=True,
    )
    my_index = me.astype(F32)
    slot_row = iota((parents, slots), 1)
    member[...] = jnp.where(
        (owner_col == my_index) & (slot_row >= first_col) & (slot_row < first_col + count_col), 1.0, 0.0
    ).astype(BF16)
    block_parent, block_live = [], []
    for dx, dc in here + far + near:
        parent, owner = owners_of_block(own_at(dx, dc, -1))
        block_parent.append(parent)
        block_live.append(owner == my_index)
    live = jnp.concatenate([jnp.where(one, 1.0, 0.0) for one in block_live], axis=0)
    rank = jnp.dot(live.astype(BF16), upper, preferred_element_type=F32)
    spot = jnp.where(live > 0.5, rank - 1.0, -1.0)
    for k in range(groups):
        chosen = spot[k:k + 1, :] == slot_iota
        parent = jnp.sum(jnp.where(chosen, block_parent[k] + 1.0, 0.0), axis=1, keepdims=True) - 1.0
        onehot[k * CAP:(k + 1) * CAP, :] = jnp.where(parent == iota((CAP, parents), 1), 1.0, 0.0).astype(BF16)

    cent_copy.wait()
    step_rows = 64

    @pl.loop(0, slots // step_rows)
    def _(i):
        span = pl.ds(pl.multiple_of(i * step_rows, step_rows), step_rows)
        cent_unit[span, :] = unit_rms(cent_raw[span, :]).astype(BF16)

    half = groups // 2
    tall = half * CAP
    scale = 1.0 / (width * 0.05)
    wide = 256
    sums = [None] * (slots // wide)
    for h in range(2):
        for k in range(h * half, (h + 1) * half):
            if k in arrivals:
                arrivals[k].wait_recv()
        span = slice(h * tall, (h + 1) * tall)
        for n in range(slots // wide):
            cols = slice(n * wide, (n + 1) * wide)
            score = lax.dot_general(
                rows[span, :], cent_unit[cols, :], (((1,), (1,)), ((), ())), preferred_element_type=F32
            )
            allowed = jnp.dot(onehot[span, :], member[:, cols], preferred_element_type=F32)
            value = jnp.where(allowed > 0.5, jnp.exp(score * scale), 0.0)
            weights[span, cols] = value
            total = jnp.sum(value, axis=0, keepdims=True)
            sums[n] = total if h == 0 else sums[n] + total
    column = jnp.concatenate(sums, axis=1)

    def column_total(sweep, local):
        ysum_send[sweep] = local
        copies = [
            send(ysum_send.at[sweep], ysum_recv.at[sweep, s - 1], ys_send.at[sweep, s - 1],
                 ys_recv.at[sweep, s - 1], dev_y(s))
            for s in range(1, ny)
        ]
        total = local
        for s, copy in enumerate(copies):
            copy.wait_recv()
            total = total + ysum_recv[sweep, s]
        zsum_send[sweep] = total
        copies = [
            send(zsum_send.at[sweep], zsum_recv.at[sweep, s - 1], zs_send.at[sweep, s - 1],
                 zs_recv.at[sweep, s - 1], dev_z(s))
            for s in range(1, nz)
        ]
        for s, copy in enumerate(copies):
            copy.wait_recv()
            total = total + zsum_recv[sweep, s]
        return total

    row_step = 128
    for sweep in range(SWEEPS):
        total = column_total(sweep, column)
        inverse = 1.0 / jnp.where(total > 0.0, total, 1.0)
        column = None
        for i in range(groups * CAP // row_step):
            span = slice(i * row_step, (i + 1) * row_step)
            value = weights[span, :] * inverse
            row_sum = jnp.sum(value, axis=1, keepdims=True)
            value = value * (1.0 / jnp.where(row_sum > 0.0, row_sum, 1.0))
            if sweep < SWEEPS - 1:
                weights[span, :] = value
                partial = jnp.sum(value, axis=0, keepdims=True)
                column = partial if column is None else column + partial
            else:
                assign_t[:, span] = jnp.transpose(value).astype(BF16)

    share = slots // (ny * nz)
    sizes = {"y": ny, "z": nz}
    places = {"y": (at_y, dev_y), "z": (at_z, dev_z)}
    steps, copies = {}, {}
    first, sem = 0, 0
    for index, (order, cols, long, mode) in enumerate(TILES):
        send1, recv1, middle, send2, recv2 = tile_bufs[5 * index:5 * index + 5]
        window = pl.ds(first, cols)

        def product(window=window, first=first, cols=cols):
            value = jnp.dot(assign_t[...], rows[:, first:first + cols], preferred_element_type=F32)
            part[:, :, :, first:first + cols] = value.reshape(ny, nz, share, cols)

        steps[index, "product"] = product
        for stage, axis in enumerate(order):
            n = sizes[axis]
            at, dev = places[axis]
            kind = "ring" if stage == 0 else mode
            send_buf, recv_buf = (send1, recv1) if stage == 0 else (send2, recv2)
            if stage == 1:
                def chunk(k, middle=middle):
                    return middle[pl.ds(k, 1)][0]
            elif axis == "y":
                def chunk(k, window=window):
                    return part[pl.ds(k, 1), :, :, window][0]
            else:
                def chunk(k, window=window):
                    return part[:, pl.ds(k, 1), :, window][:, 0]

            messages = stage_messages(kind, n, long)
            names = [(index, stage, name, step) for name, step, _, _ in messages]
            slot_of = {name: slot for slot, name in enumerate(names)}

            def put(key, value, device, slot_of=slot_of, send_buf=send_buf, recv_buf=recv_buf, sem=sem):
                slot = slot_of[key]
                send_buf[slot] = value.astype(BF16)
                copies[key] = send(
                    send_buf.at[slot], recv_buf.at[slot], rs_send.at[sem + slot], rs_recv.at[sem + slot], device
                )

            def got(key, slot_of=slot_of, recv_buf=recv_buf):
                copies[key].wait_recv()
                return recv_buf[slot_of[key]].astype(F32)

            def total(keys, at=at, chunk=chunk, got=got, stage=stage, middle=middle, first=first, cols=cols):
                value = chunk(at(0))
                for key in keys:
                    value = value + got(key)
                if stage == 0:
                    middle[...] = value
                else:
                    final[:, first:first + cols] = value

            if kind == "ring":
                for key, (name, step, way, _) in zip(names, messages):
                    last = n // 2 if name == "far" else n // 2 - 1

                    def forward(
                        key=key, step=step, way=way, last=last, at=at, dev=dev, chunk=chunk, got=got, put=put
                    ):
                        value = chunk(at(way * (last - step + 1)))
                        if step > 1:
                            value = value + got(key[:3] + (step - 1,))
                        put(key, value, dev(way))

                    steps[key] = forward
                ends = [key for key in names if key[3] == (n // 2 if key[2] == "far" else n // 2 - 1)]
            else:
                def spread(names=names, at=at, dev=dev, chunk=chunk, put=put):
                    for key in names:
                        put(key, chunk(at(key[3])), dev(key[3]))

                steps[index, stage, "all"] = spread
                ends = names
            steps[index, stage, "sum"] = functools.partial(total, ends)
            sem += n - 1
        first += cols

    for key in schedule(sizes, slots):
        steps[key]()

    base = cent_unit[pl.ds(pl.multiple_of(pts * share, share), share), :].astype(F32)
    out_ref[...] = unit_rms(base + 8.0 * final[...]).astype(BF16)
    for copy in pending:
        copy.wait_send()


def local(mesh_pts, mesh_own, points, parent_of, owner_of, child_count, centroids):
    ny = NY
    nz = mesh_pts // ny
    nx = mesh_own // CORES
    tokens, width = points.shape
    slots = centroids.shape[1]
    parents = owner_of.shape[0]
    share = slots // mesh_pts
    groups = mesh_own
    tile_shapes = []
    sems = 0
    for order, cols, _, _ in TILES:
        n1, n2 = (ny, nz) if order == "yz" else (nz, ny)
        tile_shapes += [
            pltpu.VMEM((n1 - 1, n2, share, cols), BF16),
            pltpu.VMEM((n1 - 1, n2, share, cols), BF16),
            pltpu.VMEM((n2, share, cols), F32),
            pltpu.VMEM((n2 - 1, share, cols), BF16),
            pltpu.VMEM((n2 - 1, share, cols), BF16),
        ]
        sems += n1 + n2 - 2
    dma = pltpu.SemaphoreType.DMA
    out = pl.pallas_call(
        functools.partial(kernel_entry, ny, nz, nx, len(tile_shapes)),
        out_shape=jax.ShapeDtypeStruct((share, width), BF16),
        in_specs=[pl.BlockSpec(memory_space=pltpu.VMEM)] * 4 + [pl.BlockSpec(memory_space=pl.ANY)],
        out_specs=pl.BlockSpec(memory_space=pltpu.VMEM),
        scratch_shapes=[
            pltpu.VMEM((slots, width), BF16),
            pltpu.VMEM((slots, width), BF16),
            pltpu.VMEM((tokens, width), BF16),
            pltpu.VMEM((groups * CAP, width), BF16),
            pltpu.VMEM((groups * CAP, width), BF16),
            pltpu.VMEM((parents, slots), BF16),
            pltpu.VMEM((groups * CAP, parents), BF16),
            pltpu.VMEM((groups, tokens), F32),
            pltpu.VMEM((groups * CAP, slots), F32),
            pltpu.VMEM((slots, groups * CAP), BF16),
            pltpu.VMEM((ny, nz, share, width), F32),
            pltpu.VMEM((share, width), F32),
            pltpu.VMEM((SWEEPS, 1, slots), F32),
            pltpu.VMEM((SWEEPS, ny - 1, 1, slots), F32),
            pltpu.VMEM((SWEEPS, 1, slots), F32),
            pltpu.VMEM((SWEEPS, nz - 1, 1, slots), F32),
            *tile_shapes,
            dma,
            dma((groups,)),
            dma((groups,)),
            dma((SWEEPS, ny - 1)),
            dma((SWEEPS, ny - 1)),
            dma((SWEEPS, nz - 1)),
            dma((SWEEPS, nz - 1)),
            dma((sems,)),
            dma((sems,)),
        ],
        compiler_params=pltpu.CompilerParams(
            collective_id=0, has_side_effects=True, vmem_limit_bytes=60 * 1024 * 1024
        ),
    )(
        points,
        parent_of.reshape(1, groups * tokens),
        owner_of.reshape(1, parents),
        child_count.reshape(1, parents),
        centroids[0],
    )
    return out[None]


def kernel_entry(ny, nz, nx, tiles, *refs):
    head, rest = refs[:6 + 16], refs[6 + 16:]
    return kernel(ny, nz, nx, *head, rest[:tiles], *rest[tiles:])


def solution(mesh):
    in_specs = (P(("pts", "own"), None), P("pts", None), P(), P(), P("own", None, None))
    out_specs = P("own", "pts", None)
    body = functools.partial(local, mesh.shape["pts"], mesh.shape["own"])
    return jax.shard_map(body, mesh=mesh, in_specs=in_specs, out_specs=out_specs, check_vma=False)
```

```python
import functools

import jax
import jax.numpy as jnp
from jax import lax
from jax.experimental import pallas as pl
from jax.experimental.pallas import tpu as pltpu
from jax.sharding import PartitionSpec as P

SWEEPS = 2
CAP = 64
PAIR = 96
HALF = PAIR // 2
EXTRA = CAP - HALF
CORES = 2
NY = 4
MESH = pl.DeviceIdType.MESH
F32 = jnp.float32
BF16 = jnp.bfloat16

GROUP = 256
TILES = (
    ("yz", 0, 256, -1, "direct"),
    ("zy", 1, 128, 1, "direct"),
    ("zy", 1, 128, -1, "direct"),
    ("zy", 2, 128, -1, "direct"),
    ("zy", 2, 128, 1, "direct"),
    ("yz", 3, 256, 1, "direct"),
    ("yz", 4, 128, -1, "ring"),
    ("yz", 4, 128, 1, "ring"),
    ("zy", 5, 128, -1, "direct"),
    ("zy", 5, 128, 1, "direct"),
)


def stage_messages(mode, n, long):
    far = n // 2
    if mode == "ring":
        return [("far", t, long, 1) for t in range(1, far + 1)] + [("near", t, -long, 1) for t in range(1, far)]
    return [("one", long * far, long, far)] + [
        ("one", hops * way, way, hops) for hops in range(far - 1, 0, -1) for way in (long, -long)
    ]


def tile_tasks(index, tile, sizes, slots):
    order, group, cols, long, mode = tile
    share = slots
    for axis in order:
        share //= sizes[axis]
    before = ("product", group)
    tasks = {before: ((), (), 0.68, ())}
    for stage, axis in enumerate(order):
        n = sizes[axis]
        chunk = (slots // n if stage == 0 else share) * cols
        work = chunk * 2.1e-6
        kind = "ring" if stage == 0 else mode
        messages = stage_messages(kind, n, long)
        names = [(index, stage, name, step) for name, step, _, _ in messages]
        wire = [(name, axis, way, hops, chunk * 2) for name, (_, _, way, hops) in zip(names, messages)]
        done = (index, stage, "sum")
        if kind == "ring":
            for key, one in zip(names, wire):
                last = key[:3] + (key[3] - 1,)
                first = key[3] == 1
                tasks[key] = ((before,) if first else (last,), () if first else (last,), work, (one,))
            ends = [(index, stage, "far", n // 2)] + ([(index, stage, "near", n // 2 - 1)] if n > 2 else [])
            tasks[done] = (tuple(ends), tuple(ends), 2 * work, ())
        else:
            tasks[index, stage, "all"] = ((before,), (), n * work, tuple(wire))
            tasks[done] = (((index, stage, "all"),), tuple(names), n * work, ())
        before = done
    return tasks


def schedule(sizes, slots):
    rate, hop_us, next_hop_us = 46500.0, 2.2, 0.75
    tasks = {}
    for index, tile in enumerate(TILES):
        tasks.update(tile_tasks(index, tile, sizes, slots))
    sender = {message[0]: key for key, task in tasks.items() for message in task[3]}
    after = {key: [] for key in tasks}
    for key, (before, waits, _, _) in tasks.items():
        for one in before:
            after[one].append((key, 0.0))
        for one in waits:
            after[sender[one]].append((key, hop_us))
    chain = {}

    def length(key):
        if key not in chain:
            chain[key] = tasks[key][2] + max([gap + length(one) for one, gap in after[key]], default=0.0)
        return chain[key]

    now, order, arrival, link_free, done = 0.0, [], {}, {}, set()
    while len(order) < len(tasks):
        ready = []
        for key, (before, waits, _, _) in tasks.items():
            if key not in done and all(one in done for one in before) and all(one in arrival for one in waits):
                ready.append((max([arrival[one] for one in waits], default=0.0), key))
        started = [one for one in ready if one[0] <= now]
        if started:
            at, key = max(started, key=lambda one: length(one[1]))
        else:
            at, key = min(ready, key=lambda one: (one[0], -length(one[1])))
        now = max(now, at) + tasks[key][2]
        for name, axis, way, hops, size in tasks[key][3]:
            start = max(now, link_free.get((axis, way), 0.0))
            link_free[axis, way] = start + hops * size / rate
            arrival[name] = link_free[axis, way] + hop_us + next_hop_us * (hops - 1)
        done.add(key)
        order.append(key)
    return order


def unit_rms(values):
    values = values.astype(F32)
    return values * lax.rsqrt(jnp.mean(values * values, axis=-1, keepdims=True) + 1e-06)


def iota(shape, dim):
    return lax.broadcasted_iota(jnp.int32, shape, dim).astype(F32)


def kernel(
    ny, nz, nx,
    points_hbm, parent_ref, owner_ref, count_ref, cent_hbm, out_ref,
    point_raw, cent_raw, cent_unit, point_unit, packed, rows, member, onehot, place, weights, assign_t, part, final,
    ysum_send, ysum_recv, zsum_send, zsum_recv, tile_bufs,
    point_sem, cent_sem, x_send, x_recv, f_send, f_recv, ys_send, ys_recv, zs_send, zs_recv, rs_send, rs_recv,
):
    pts, me = lax.axis_index("pts"), lax.axis_index("own")
    y, z = lax.div(pts, nz), lax.rem(pts, nz)
    x, core = lax.div(me, CORES), lax.rem(me, CORES)
    groups = nx * CORES
    tokens, width = points_hbm.shape
    parents = owner_ref.shape[1]
    slots = cent_hbm.shape[0]

    def own_at(dx, dc, sign):
        other = lax.rem(x + (dx if sign > 0 else nx - dx), nx)
        return other * CORES + (core if dc == 0 else 1 - core)

    def at_y(step):
        return lax.rem(y + step + ny, ny)

    def at_z(step):
        return lax.rem(z + step + nz, nz)

    def dev_y(step):
        return (at_y(step) * nz + z, me)

    def dev_z(step):
        return (y * nz + at_z(step), me)

    offsets = [(dx, dc) for dx in range(nx) for dc in range(CORES)]
    barrier = pltpu.get_barrier_semaphore()
    peers = [(pts, own_at(dx, dc, 1)) for dx, dc in offsets if (dx, dc) != (0, 0)]
    peers += [dev_y(s) for s in range(1, ny)] + [dev_z(s) for s in range(1, nz)]
    for peer in peers:
        pl.semaphore_signal(barrier, inc=1, device_id=peer, device_id_type=MESH)
    point_copy = pltpu.make_async_copy(points_hbm, point_raw, point_sem)
    point_copy.start()
    cent_copy = pltpu.make_async_copy(cent_hbm, cent_raw, cent_sem)
    cent_copy.start()

    pending = []

    def send(src, dst, send_sem, recv_sem, device):
        copy = pltpu.make_async_remote_copy(
            src_ref=src, dst_ref=dst, send_sem=send_sem, recv_sem=recv_sem,
            device_id=device, device_id_type=MESH,
        )
        copy.start()
        pending.append(copy)
        return copy

    square = (parents, parents)
    owner_row = owner_ref[...].astype(F32)
    count_row = count_ref[...].astype(F32)
    diagonal = iota(square, 0) == iota(square, 1)
    owner_col = jnp.sum(jnp.where(diagonal, owner_row, 0.0), axis=1, keepdims=True)
    count_col = jnp.sum(jnp.where(diagonal, count_row, 0.0), axis=1, keepdims=True)
    upper = jnp.where(iota((tokens, tokens), 0) <= iota((tokens, tokens), 1), 1.0, 0.0).astype(BF16)
    parent_iota = iota((parents, tokens), 0)

    def owners_of_block(index):
        parent = parent_ref[:, pl.ds(pl.multiple_of(index * tokens, tokens), tokens)].astype(F32)
        return parent, jnp.sum(jnp.where(parent_iota == parent, owner_col, 0.0), axis=0, keepdims=True)

    _, my_owner = owners_of_block(me)
    goes = my_owner == iota((groups, tokens), 0)
    rank = jnp.dot(jnp.where(goes, 1.0, 0.0).astype(BF16), upper, preferred_element_type=F32)
    odd = lax.rem(lax.broadcasted_iota(jnp.int32, (groups, tokens), 0), CORES) == 1
    place[...] = jnp.where(goes, jnp.where(odd, PAIR - rank, rank - 1.0), -1.0)
    point_copy.wait()
    point_unit[...] = unit_rms(point_raw[...]).astype(BF16)

    pair_iota = iota((PAIR, tokens), 0)
    near, far = (1, nx - 1), (nx // 2,)
    blocks = [(dx, dc) for dx in (0,) + near + far for dc in range(CORES)]
    block_of = {offset: i for i, offset in enumerate(blocks)}

    def pack(group):
        picks = []
        for dx in group:
            chip = lax.rem(x + dx, nx) * CORES
            taken = place[pl.ds(chip, 1), :] == pair_iota
            for other in range(1, CORES):
                taken = taken | (place[pl.ds(chip + other, 1), :] == pair_iota)
            picks.append(jnp.where(taken, 1.0, 0.0).astype(BF16))
        block = jnp.dot(jnp.concatenate(picks, axis=0), point_unit[...], preferred_element_type=F32).astype(BF16)
        for i, dx in enumerate(group):
            packed[dx * PAIR:(dx + 1) * PAIR, :] = block[i * PAIR:(i + 1) * PAIR]

    def part_of(start, size):
        return pl.ds(pl.multiple_of(start, EXTRA), size)

    arrivals, forwards = {}, {}

    def depart(dx):
        for dc in range(CORES):
            k = block_of[dx, dc]
            to_core = core if dc == 0 else 1 - core
            arrivals[dx, dc] = send(
                packed.at[part_of(dx * PAIR + HALF * to_core, HALF)], rows.at[part_of(k * CAP + EXTRA * to_core, HALF)],
                x_send.at[k], x_recv.at[k], (pts, own_at(dx, dc, 1)),
            )

    def hand_over(dx, dc):
        k, other = block_of[dx, dc], block_of[dx, 1 - dc]
        arrivals[dx, dc].wait_recv()
        forwards[dx, dc] = send(
            rows.at[part_of(k * CAP + 2 * EXTRA - EXTRA * core, EXTRA)], rows.at[part_of(other * CAP + HALF * core, EXTRA)],
            f_send.at[k], f_recv.at[other], (pts, own_at(0, 1, 1)),
        )

    pack(near)
    pl.semaphore_wait(barrier, len(peers))
    for dx in near:
        depart(dx)
    pack(far)
    for dx in far:
        depart(dx)
    pack((0,))
    mine, theirs = block_of[0, 0], block_of[0, 1]
    rows[mine * CAP:(mine + 1) * CAP, :] = packed[part_of((PAIR - CAP) * core, CAP), :]
    arrivals[0, 1] = send(
        packed.at[part_of((PAIR - CAP) * (1 - core), CAP)], rows.at[pl.ds(theirs * CAP, CAP)],
        x_send.at[theirs], x_recv.at[theirs], (pts, own_at(0, 1, 1)),
    )

    first_col = jnp.sum(
        jnp.where((owner_col == owner_row) & (iota(square, 1) < iota(square, 0)), count_row, 0.0),
        axis=1, keepdims=True,
    )
    my_index = me.astype(F32)
    slot_row = iota((parents, slots), 1)
    member[...] = jnp.where(
        (owner_col == my_index) & (slot_row >= first_col) & (slot_row < first_col + count_col), 1.0, 0.0
    ).astype(BF16)
    block_parent, block_live = [], []
    for dx, dc in blocks:
        parent, owner = owners_of_block(own_at(dx, dc, -1))
        block_parent.append(parent)
        block_live.append(owner == my_index)
    live = jnp.concatenate([jnp.where(one, 1.0, 0.0) for one in block_live], axis=0)
    rank = jnp.dot(live.astype(BF16), upper, preferred_element_type=F32)
    spot = jnp.where(live > 0.5, rank - 1.0, -1.0)
    slot_iota = iota((CAP, tokens), 0)
    slot_iota = jnp.where(core == 0, slot_iota, (CAP - 1.0) - slot_iota)
    for k in range(groups):
        chosen = spot[k:k + 1, :] == slot_iota
        parent = jnp.sum(jnp.where(chosen, block_parent[k] + 1.0, 0.0), axis=1, keepdims=True) - 1.0
        onehot[k * CAP:(k + 1) * CAP, :] = jnp.where(parent == iota((CAP, parents), 1), 1.0, 0.0).astype(BF16)

    cent_copy.wait()
    step_rows = 64

    @pl.loop(0, slots // step_rows)
    def _(i):
        span = pl.ds(pl.multiple_of(i * step_rows, step_rows), step_rows)
        cent_unit[span, :] = unit_rms(cent_raw[span, :]).astype(BF16)

    scale = 1.0 / (width * 0.05)
    wide = 256
    sums = [None] * (slots // wide)
    done = 0
    for stage in (near, far):
        for dx in stage:
            for dc in range(CORES):
                hand_over(dx, dc)
        if stage is near:
            arrivals[0, 1].wait_recv()
        for dx in stage:
            for dc in range(CORES):
                forwards[dx, dc].wait_recv()
        ready = done + (len(stage) + (1 if stage is near else 0)) * CORES * CAP
        span = slice(done, ready)
        for n in range(slots // wide):
            cols = slice(n * wide, (n + 1) * wide)
            score = lax.dot_general(
                rows[span, :], cent_unit[cols, :], (((1,), (1,)), ((), ())), preferred_element_type=F32
            )
            allowed = jnp.dot(onehot[span, :], member[:, cols], preferred_element_type=F32)
            value = jnp.where(allowed > 0.5, jnp.exp(score * scale), 0.0)
            weights[span, cols] = value
            total = jnp.sum(value, axis=0, keepdims=True)
            sums[n] = total if done == 0 else sums[n] + total
        done = ready
    column = jnp.concatenate(sums, axis=1)

    def column_total(sweep, local):
        ysum_send[sweep] = local
        copies = [
            send(ysum_send.at[sweep], ysum_recv.at[sweep, s - 1], ys_send.at[sweep, s - 1],
                 ys_recv.at[sweep, s - 1], dev_y(s))
            for s in range(1, ny)
        ]
        total = local
        for s, copy in enumerate(copies):
            copy.wait_recv()
            total = total + ysum_recv[sweep, s]
        zsum_send[sweep] = total
        copies = [
            send(zsum_send.at[sweep], zsum_recv.at[sweep, s - 1], zs_send.at[sweep, s - 1],
                 zs_recv.at[sweep, s - 1], dev_z(s))
            for s in range(1, nz)
        ]
        for s, copy in enumerate(copies):
            copy.wait_recv()
            total = total + zsum_recv[sweep, s]
        return total

    row_step = 128
    for sweep in range(SWEEPS):
        total = column_total(sweep, column)
        inverse = 1.0 / jnp.where(total > 0.0, total, 1.0)
        column = None
        for i in range(groups * CAP // row_step):
            span = slice(i * row_step, (i + 1) * row_step)
            value = weights[span, :] * inverse
            row_sum = jnp.sum(value, axis=1, keepdims=True)
            value = value * (1.0 / jnp.where(row_sum > 0.0, row_sum, 1.0))
            if sweep < SWEEPS - 1:
                weights[span, :] = value
                partial = jnp.sum(value, axis=0, keepdims=True)
                column = partial if column is None else column + partial
            else:
                assign_t[:, span] = jnp.transpose(value).astype(BF16)

    share = slots // (ny * nz)
    sizes = {"y": ny, "z": nz}
    places = {"y": (at_y, dev_y), "z": (at_z, dev_z)}
    steps, copies = {}, {}
    sem = 0
    taken_columns = [group * GROUP for group in range(width // GROUP)]
    for group in {tile[1] for tile in TILES}:
        def product(span=slice(group * GROUP, (group + 1) * GROUP)):
            value = jnp.dot(assign_t[...], rows[:, span], preferred_element_type=F32)
            part[:, :, :, span] = value.reshape(ny, nz, share, GROUP)

        steps["product", group] = product
    for index, (order, group_of, cols, long, mode) in enumerate(TILES):
        send1, recv1, middle, send2, recv2 = tile_bufs[5 * index:5 * index + 5]
        first = taken_columns[group_of]
        taken_columns[group_of] += cols
        window = pl.ds(first, cols)

        for stage, axis in enumerate(order):
            n = sizes[axis]
            at, dev = places[axis]
            kind = "ring" if stage == 0 else mode
            send_buf, recv_buf = (send1, recv1) if stage == 0 else (send2, recv2)
            if stage == 1:
                def chunk(k, middle=middle):
                    return middle[pl.ds(k, 1)][0]
            elif axis == "y":
                def chunk(k, window=window):
                    return part[pl.ds(k, 1), :, :, window][0]
            else:
                def chunk(k, window=window):
                    return part[:, pl.ds(k, 1), :, window][:, 0]

            messages = stage_messages(kind, n, long)
            names = [(index, stage, name, step) for name, step, _, _ in messages]
            slot_of = {name: slot for slot, name in enumerate(names)}

            def put(key, value, device, slot_of=slot_of, send_buf=send_buf, recv_buf=recv_buf, sem=sem):
                slot = slot_of[key]
                send_buf[slot] = value.astype(BF16)
                copies[key] = send(
                    send_buf.at[slot], recv_buf.at[slot], rs_send.at[sem + slot], rs_recv.at[sem + slot], device
                )

            def got(key, slot_of=slot_of, recv_buf=recv_buf):
                copies[key].wait_recv()
                return recv_buf[slot_of[key]].astype(F32)

            def total(keys, at=at, chunk=chunk, got=got, stage=stage, middle=middle, first=first, cols=cols):
                value = chunk(at(0))
                for key in keys:
                    value = value + got(key)
                if stage == 0:
                    middle[...] = value
                else:
                    final[:, first:first + cols] = value

            if kind == "ring":
                for key, (name, step, way, _) in zip(names, messages):
                    last = n // 2 if name == "far" else n // 2 - 1

                    def forward(
                        key=key, step=step, way=way, last=last, at=at, dev=dev, chunk=chunk, got=got, put=put
                    ):
                        value = chunk(at(way * (last - step + 1)))
                        if step > 1:
                            value = value + got(key[:3] + (step - 1,))
                        put(key, value, dev(way))

                    steps[key] = forward
                ends = [key for key in names if key[3] == (n // 2 if key[2] == "far" else n // 2 - 1)]
            else:
                def spread(names=names, at=at, dev=dev, chunk=chunk, put=put):
                    for key in names:
                        put(key, chunk(at(key[3])), dev(key[3]))

                steps[index, stage, "all"] = spread
                ends = names
            steps[index, stage, "sum"] = functools.partial(total, ends)
            sem += n - 1

    for key in schedule(sizes, slots):
        steps[key]()

    base = cent_unit[pl.ds(pl.multiple_of(pts * share, share), share), :].astype(F32)
    out_ref[...] = unit_rms(base + 8.0 * final[...]).astype(BF16)
    for copy in pending:
        copy.wait_send()


def local(mesh_pts, mesh_own, points, parent_of, owner_of, child_count, centroids):
    ny = NY
    nz = mesh_pts // ny
    nx = mesh_own // CORES
    tokens, width = points.shape
    slots = centroids.shape[1]
    parents = owner_of.shape[0]
    share = slots // mesh_pts
    groups = mesh_own
    tile_shapes = []
    sems = 0
    for order, _, cols, _, _ in TILES:
        n1, n2 = (ny, nz) if order == "yz" else (nz, ny)
        tile_shapes += [
            pltpu.VMEM((n1 - 1, n2, share, cols), BF16),
            pltpu.VMEM((n1 - 1, n2, share, cols), BF16),
            pltpu.VMEM((n2, share, cols), F32),
            pltpu.VMEM((n2 - 1, share, cols), BF16),
            pltpu.VMEM((n2 - 1, share, cols), BF16),
        ]
        sems += n1 + n2 - 2
    dma = pltpu.SemaphoreType.DMA
    out = pl.pallas_call(
        functools.partial(kernel_entry, ny, nz, nx, len(tile_shapes)),
        out_shape=jax.ShapeDtypeStruct((share, width), BF16),
        in_specs=[pl.BlockSpec(memory_space=pl.ANY)]
        + [pl.BlockSpec(memory_space=pltpu.VMEM)] * 3
        + [pl.BlockSpec(memory_space=pl.ANY)],
        out_specs=pl.BlockSpec(memory_space=pltpu.VMEM),
        scratch_shapes=[
            pltpu.VMEM((tokens, width), BF16),
            pltpu.VMEM((slots, width), BF16),
            pltpu.VMEM((slots, width), BF16),
            pltpu.VMEM((tokens, width), BF16),
            pltpu.VMEM((nx * PAIR, width), BF16),
            pltpu.VMEM((groups * CAP, width), BF16),
            pltpu.VMEM((parents, slots), BF16),
            pltpu.VMEM((groups * CAP, parents), BF16),
            pltpu.VMEM((groups, tokens), F32),
            pltpu.VMEM((groups * CAP, slots), F32),
            pltpu.VMEM((slots, groups * CAP), BF16),
            pltpu.VMEM((ny, nz, share, width), F32),
            pltpu.VMEM((share, width), F32),
            pltpu.VMEM((SWEEPS, 1, slots), F32),
            pltpu.VMEM((SWEEPS, ny - 1, 1, slots), F32),
            pltpu.VMEM((SWEEPS, 1, slots), F32),
            pltpu.VMEM((SWEEPS, nz - 1, 1, slots), F32),
            *tile_shapes,
            dma,
            dma,
            dma((groups,)),
            dma((groups,)),
            dma((groups,)),
            dma((groups,)),
            dma((SWEEPS, ny - 1)),
            dma((SWEEPS, ny - 1)),
            dma((SWEEPS, nz - 1)),
            dma((SWEEPS, nz - 1)),
            dma((sems,)),
            dma((sems,)),
        ],
        compiler_params=pltpu.CompilerParams(
            collective_id=0, has_side_effects=True, vmem_limit_bytes=60 * 1024 * 1024
        ),
    )(
        points,
        parent_of.reshape(1, groups * tokens),
        owner_of.reshape(1, parents),
        child_count.reshape(1, parents),
        centroids[0],
    )
    return out[None]


def kernel_entry(ny, nz, nx, tiles, *refs):
    head, rest = refs[:6 + 17], refs[6 + 17:]
    return kernel(ny, nz, nx, *head, rest[:tiles], *rest[tiles:])


def solution(mesh):
    in_specs = (P(("pts", "own"), None), P("pts", None), P(), P(), P("own", None, None))
    out_specs = P("own", "pts", None)
    body = functools.partial(local, mesh.shape["pts"], mesh.shape["own"])
    return jax.shard_map(body, mesh=mesh, in_specs=in_specs, out_specs=out_specs, check_vma=False)
```

```python
import functools

import jax
import jax.numpy as jnp
from jax import lax
from jax.experimental import pallas as pl
from jax.experimental.pallas import tpu as pltpu
from jax.sharding import PartitionSpec as P

SWEEPS = 2
CAP = 64
PAIR = 96
HALF = PAIR // 2
EXTRA = CAP - HALF
LAST = 384
CORES = 2
NY = 4
MESH = pl.DeviceIdType.MESH
F32 = jnp.float32
BF16 = jnp.bfloat16

GROUP = 256
TILES = (
    ("yz", 0, 256, -1, "direct"),
    ("zy", 1, 128, 1, "direct"),
    ("zy", 1, 128, -1, "direct"),
    ("zy", 2, 128, -1, "direct"),
    ("zy", 2, 128, 1, "direct"),
    ("yz", 3, 256, 1, "direct"),
    ("yz", 4, 128, -1, "ring"),
    ("yz", 4, 128, 1, "ring"),
    ("zy", 5, 128, -1, "direct"),
    ("zy", 5, 128, 1, "direct"),
)


def stage_messages(mode, n, long):
    far = n // 2
    if mode == "ring":
        return [("far", t, long, 1) for t in range(1, far + 1)] + [("near", t, -long, 1) for t in range(1, far)]
    return [("one", long * far, long, far)] + [
        ("one", hops * way, way, hops) for hops in range(far - 1, 0, -1) for way in (long, -long)
    ]


def tile_tasks(index, tile, sizes, slots):
    order, group, cols, long, mode = tile
    share = slots
    for axis in order:
        share //= sizes[axis]
    before = ("product", group)
    tasks = {before: ((), (), 0.68, ())}
    for stage, axis in enumerate(order):
        n = sizes[axis]
        chunk = (slots // n if stage == 0 else share) * cols
        work = chunk * 2.1e-6
        kind = "ring" if stage == 0 else mode
        messages = stage_messages(kind, n, long)
        names = [(index, stage, name, step) for name, step, _, _ in messages]
        wire = [(name, axis, way, hops, chunk * 2) for name, (_, _, way, hops) in zip(names, messages)]
        done = (index, stage, "sum")
        if kind == "ring":
            for key, one in zip(names, wire):
                last = key[:3] + (key[3] - 1,)
                first = key[3] == 1
                tasks[key] = ((before,) if first else (last,), () if first else (last,), work, (one,))
            ends = [(index, stage, "far", n // 2)] + ([(index, stage, "near", n // 2 - 1)] if n > 2 else [])
            tasks[done] = (tuple(ends), tuple(ends), 2 * work, ())
        else:
            tasks[index, stage, "all"] = ((before,), (), n * work, tuple(wire))
            tasks[done] = (((index, stage, "all"),), tuple(names), n * work, ())
        before = done
    return tasks


def schedule(sizes, slots):
    rate, hop_us, next_hop_us = 46500.0, 2.2, 0.75
    tasks = {}
    for index, tile in enumerate(TILES):
        tasks.update(tile_tasks(index, tile, sizes, slots))
    sender = {message[0]: key for key, task in tasks.items() for message in task[3]}
    after = {key: [] for key in tasks}
    for key, (before, waits, _, _) in tasks.items():
        for one in before:
            after[one].append((key, 0.0))
        for one in waits:
            after[sender[one]].append((key, hop_us))
    chain = {}

    def length(key):
        if key not in chain:
            chain[key] = tasks[key][2] + max([gap + length(one) for one, gap in after[key]], default=0.0)
        return chain[key]

    now, order, arrival, link_free, done = 0.0, [], {}, {}, set()
    while len(order) < len(tasks):
        ready = []
        for key, (before, waits, _, _) in tasks.items():
            if key not in done and all(one in done for one in before) and all(one in arrival for one in waits):
                ready.append((max([arrival[one] for one in waits], default=0.0), key))
        started = [one for one in ready if one[0] <= now]
        if started:
            at, key = max(started, key=lambda one: length(one[1]))
        else:
            at, key = min(ready, key=lambda one: (one[0], -length(one[1])))
        now = max(now, at) + tasks[key][2]
        for name, axis, way, hops, size in tasks[key][3]:
            start = max(now, link_free.get((axis, way), 0.0))
            link_free[axis, way] = start + hops * size / rate
            arrival[name] = link_free[axis, way] + hop_us + next_hop_us * (hops - 1)
        done.add(key)
        order.append(key)
    return order


def unit_rms(values):
    values = values.astype(F32)
    return values * lax.rsqrt(jnp.mean(values * values, axis=-1, keepdims=True) + 1e-06)


def iota(shape, dim):
    return lax.broadcasted_iota(jnp.int32, shape, dim).astype(F32)


def kernel(
    ny, nz, nx,
    points_hbm, parent_ref, owner_ref, count_ref, cent_hbm, out_ref,
    point_raw, cent_raw, cent_unit, point_unit, packed, rows, member, onehot, place, weights, assign_t, part, final,
    sum_send, sum_recv, tile_bufs,
    point_sem, cent_sem, x_send, x_recv, l_send, l_recv, f_send, f_recv, s_send, s_recv, rs_send, rs_recv,
    round_sem,
):
    pts, me = lax.axis_index("pts"), lax.axis_index("own")
    y, z = lax.div(pts, nz), lax.rem(pts, nz)
    x, core = lax.div(me, CORES), lax.rem(me, CORES)
    groups = nx * CORES
    tokens, width = points_hbm.shape
    parents = owner_ref.shape[1]
    slots = cent_hbm.shape[0]

    def own_at(dx, dc, sign):
        other = lax.rem(x + (dx if sign > 0 else nx - dx), nx)
        return other * CORES + (core if dc == 0 else 1 - core)

    def at_y(step):
        return lax.rem(y + step + ny, ny)

    def at_z(step):
        return lax.rem(z + step + nz, nz)

    def dev_y(step):
        return (at_y(step) * nz + z, me)

    def dev_z(step):
        return (y * nz + at_z(step), me)

    offsets = [(dx, dc) for dx in range(nx) for dc in range(CORES)]
    barrier = pltpu.get_barrier_semaphore()
    peers = [(pts, own_at(dx, dc, 1)) for dx, dc in offsets if (dx, dc) != (0, 0)]
    peers += [dev_y(s) for s in range(1, ny)] + [dev_z(1), dev_z(-1)]
    for peer in peers:
        pl.semaphore_signal(barrier, inc=1, device_id=peer, device_id_type=MESH)
    point_copy = pltpu.make_async_copy(points_hbm, point_raw, point_sem)
    point_copy.start()
    cent_copy = pltpu.make_async_copy(cent_hbm, cent_raw, cent_sem)
    cent_copy.start()

    pending = []

    def send(src, dst, send_sem, recv_sem, device):
        copy = pltpu.make_async_remote_copy(
            src_ref=src, dst_ref=dst, send_sem=send_sem, recv_sem=recv_sem,
            device_id=device, device_id_type=MESH,
        )
        copy.start()
        pending.append(copy)
        return copy

    square = (parents, parents)
    owner_row = owner_ref[...].astype(F32)
    count_row = count_ref[...].astype(F32)
    diagonal = iota(square, 0) == iota(square, 1)
    owner_col = jnp.sum(jnp.where(diagonal, owner_row, 0.0), axis=1, keepdims=True)
    count_col = jnp.sum(jnp.where(diagonal, count_row, 0.0), axis=1, keepdims=True)
    upper = jnp.where(iota((tokens, tokens), 0) <= iota((tokens, tokens), 1), 1.0, 0.0).astype(BF16)
    parent_iota = iota((parents, tokens), 0)

    def owners_of_block(index):
        parent = parent_ref[:, pl.ds(pl.multiple_of(index * tokens, tokens), tokens)].astype(F32)
        return parent, jnp.sum(jnp.where(parent_iota == parent, owner_col, 0.0), axis=0, keepdims=True)

    _, my_owner = owners_of_block(me)
    goes = my_owner == iota((groups, tokens), 0)
    rank = jnp.dot(jnp.where(goes, 1.0, 0.0).astype(BF16), upper, preferred_element_type=F32)
    odd = lax.rem(lax.broadcasted_iota(jnp.int32, (groups, tokens), 0), CORES) == 1
    place[...] = jnp.where(goes, jnp.where(odd, PAIR - rank, rank - 1.0), -1.0)
    point_copy.wait()
    point_unit[...] = unit_rms(point_raw[...]).astype(BF16)

    pair_iota = iota((PAIR, tokens), 0)
    near, far = (1, nx - 1), (nx // 2,)
    blocks = [(dx, dc) for dx in (0,) + far + near for dc in range(CORES)]
    block_of = {offset: i for i, offset in enumerate(blocks)}

    def pack(group):
        picks = []
        for dx in group:
            chip = lax.rem(x + dx, nx) * CORES
            taken = place[pl.ds(chip, 1), :] == pair_iota
            for other in range(1, CORES):
                taken = taken | (place[pl.ds(chip + other, 1), :] == pair_iota)
            picks.append(jnp.where(taken, 1.0, 0.0).astype(BF16))
        block = jnp.dot(jnp.concatenate(picks, axis=0), point_unit[...], preferred_element_type=F32).astype(BF16)
        for i, dx in enumerate(group):
            packed[dx * PAIR:(dx + 1) * PAIR, :] = block[i * PAIR:(i + 1) * PAIR]

    def part_of(start, size):
        return pl.ds(pl.multiple_of(start, EXTRA), size)

    arrivals, lasts, forwards = {}, {}, {}

    early, late = slice(0, width - LAST), slice(width - LAST, width)

    def depart(group):
        for window in (early, late):
            for dx in group:
                for dc in range(CORES):
                    k = block_of[dx, dc]
                    to_core = core if dc == 0 else 1 - core
                    device = (pts, own_at(dx, dc, 1))
                    span = slice(0, width) if group is far else window
                    if window is early:
                        arrivals[dx, dc] = send(
                            packed.at[part_of(dx * PAIR + HALF * to_core, HALF), span],
                            rows.at[part_of(k * CAP + EXTRA * to_core, HALF), span],
                            x_send.at[k], x_recv.at[k], device,
                        )
                    elif group is near:
                        lasts[dx, dc] = send(
                            packed.at[part_of(dx * PAIR + (PAIR - CAP) * to_core, CAP), span],
                            rows.at[pl.ds(k * CAP, CAP), span],
                            l_send.at[k], l_recv.at[k], device,
                        )

    def hand_over(group, span):
        for dx in group:
            for dc in range(CORES):
                k, other = block_of[dx, dc], block_of[dx, 1 - dc]
                arrivals[dx, dc].wait_recv()
                forwards[dx, dc] = send(
                    rows.at[part_of(k * CAP + 2 * EXTRA - EXTRA * core, EXTRA), span],
                    rows.at[part_of(other * CAP + HALF * core, EXTRA), span],
                    f_send.at[k], f_recv.at[other], (pts, own_at(0, 1, 1)),
                )

    def handed_over(group):
        for dx in group:
            for dc in range(CORES):
                forwards[dx, dc].wait_recv()

    pack(far)
    pl.semaphore_wait(barrier, len(peers))
    for step in (1, -1):
        pl.semaphore_signal(round_sem.at[0], inc=1, device_id=dev_z(step), device_id_type=MESH)
    depart(far)
    pack(near)
    depart(near)
    pack((0,))
    mine, theirs = block_of[0, 0], block_of[0, 1]
    rows[mine * CAP:(mine + 1) * CAP, :] = packed[part_of((PAIR - CAP) * core, CAP), :]
    arrivals[0, 1] = send(
        packed.at[part_of((PAIR - CAP) * (1 - core), CAP)], rows.at[pl.ds(theirs * CAP, CAP)],
        x_send.at[theirs], x_recv.at[theirs], (pts, own_at(0, 1, 1)),
    )

    first_col = jnp.sum(
        jnp.where((owner_col == owner_row) & (iota(square, 1) < iota(square, 0)), count_row, 0.0),
        axis=1, keepdims=True,
    )
    my_index = me.astype(F32)
    slot_row = iota((parents, slots), 1)
    member[...] = jnp.where(
        (owner_col == my_index) & (slot_row >= first_col) & (slot_row < first_col + count_col), 1.0, 0.0
    ).astype(BF16)
    block_parent, block_live = [], []
    for dx, dc in blocks:
        parent, owner = owners_of_block(own_at(dx, dc, -1))
        block_parent.append(parent)
        block_live.append(owner == my_index)
    live = jnp.concatenate([jnp.where(one, 1.0, 0.0) for one in block_live], axis=0)
    rank = jnp.dot(live.astype(BF16), upper, preferred_element_type=F32)
    spot = jnp.where(live > 0.5, rank - 1.0, -1.0)
    slot_iota = iota((CAP, tokens), 0)
    slot_iota = jnp.where(core == 0, slot_iota, (CAP - 1.0) - slot_iota)
    for k in range(groups):
        chosen = spot[k:k + 1, :] == slot_iota
        parent = jnp.sum(jnp.where(chosen, block_parent[k] + 1.0, 0.0), axis=1, keepdims=True) - 1.0
        onehot[k * CAP:(k + 1) * CAP, :] = jnp.where(parent == iota((CAP, parents), 1), 1.0, 0.0).astype(BF16)

    cent_copy.wait()
    step_rows = 64

    @pl.loop(0, slots // step_rows)
    def _(i):
        span = pl.ds(pl.multiple_of(i * step_rows, step_rows), step_rows)
        cent_unit[span, :] = unit_rms(cent_raw[span, :]).astype(BF16)

    pl.semaphore_wait(round_sem.at[0], 2)
    for step in (2, -2):
        pl.semaphore_signal(round_sem.at[1], inc=1, device_id=dev_z(step), device_id_type=MESH)

    scale = 1.0 / (width * 0.05)
    wide = 256

    def score(span, cols, depth):
        return lax.dot_general(
            rows[span, depth], cent_unit[cols, depth], (((1,), (1,)), ((), ())), preferred_element_type=F32
        )

    def weigh(span, cols, value):
        allowed = jnp.dot(onehot[span, :], member[:, cols], preferred_element_type=F32)
        value = jnp.where(allowed > 0.5, jnp.exp(value * scale), 0.0)
        weights[span, cols] = value
        return jnp.sum(value, axis=0, keepdims=True)

    first_rows = (1 + len(far)) * CORES * CAP
    top, bottom = slice(0, first_rows), slice(first_rows, groups * CAP)
    slot_cols = [slice(n * wide, (n + 1) * wide) for n in range(slots // wide)]
    arrivals[0, 1].wait_recv()
    hand_over(far, slice(0, width))
    handed_over(far)
    sums = [weigh(top, cols, score(top, cols, slice(0, width))) for cols in slot_cols]
    pl.semaphore_wait(round_sem.at[1], 2)
    for step in (1, -1):
        pl.semaphore_signal(round_sem.at[2], inc=1, device_id=dev_z(step), device_id_type=MESH)
    hand_over(near, early)
    handed_over(near)
    for cols in slot_cols:
        weights[bottom, cols] = score(bottom, cols, early)
    for dx in near:
        for dc in range(CORES):
            lasts[dx, dc].wait_recv()
    for n, cols in enumerate(slot_cols):
        sums[n] = sums[n] + weigh(bottom, cols, weights[bottom, cols] + score(bottom, cols, late))
    column = jnp.concatenate(sums, axis=1)
    pl.semaphore_wait(round_sem.at[2], 2)

    plane = sorted(
        ((dy, dz) for dy in range(ny) for dz in range(nz) if (dy, dz) != (0, 0)),
        key=lambda one: -min(one[0], ny - one[0]) - min(one[1], nz - one[1]),
    )

    def column_total(sweep, local):
        sum_send[sweep] = local
        copies = [
            send(sum_send.at[sweep], sum_recv.at[sweep, k], s_send.at[sweep, k], s_recv.at[sweep, k],
                 (at_y(dy) * nz + at_z(dz), me))
            for k, (dy, dz) in enumerate(plane)
        ]
        total = local
        for k, copy in reversed(list(enumerate(copies))):
            copy.wait_recv()
            total = total + sum_recv[sweep, k]
        return total

    row_step = 128
    for sweep in range(SWEEPS):
        total = column_total(sweep, column)
        inverse = 1.0 / jnp.where(total > 0.0, total, 1.0)
        column = None
        for i in range(groups * CAP // row_step):
            span = slice(i * row_step, (i + 1) * row_step)
            value = weights[span, :] * inverse
            row_sum = jnp.sum(value, axis=1, keepdims=True)
            value = value * (1.0 / jnp.where(row_sum > 0.0, row_sum, 1.0))
            if sweep < SWEEPS - 1:
                weights[span, :] = value
                partial = jnp.sum(value, axis=0, keepdims=True)
                column = partial if column is None else column + partial
            else:
                assign_t[:, span] = jnp.transpose(value).astype(BF16)

    share = slots // (ny * nz)
    sizes = {"y": ny, "z": nz}
    places = {"y": (at_y, dev_y), "z": (at_z, dev_z)}
    steps, copies = {}, {}
    sem = 0
    taken_columns = [group * GROUP for group in range(width // GROUP)]
    for group in {tile[1] for tile in TILES}:
        def product(span=slice(group * GROUP, (group + 1) * GROUP)):
            value = jnp.dot(assign_t[...], rows[:, span], preferred_element_type=F32)
            part[:, :, :, span] = value.reshape(ny, nz, share, GROUP)

        steps["product", group] = product
    for index, (order, group_of, cols, long, mode) in enumerate(TILES):
        send1, recv1, middle, send2, recv2 = tile_bufs[5 * index:5 * index + 5]
        first = taken_columns[group_of]
        taken_columns[group_of] += cols
        window = pl.ds(first, cols)

        for stage, axis in enumerate(order):
            n = sizes[axis]
            at, dev = places[axis]
            kind = "ring" if stage == 0 else mode
            send_buf, recv_buf = (send1, recv1) if stage == 0 else (send2, recv2)
            if stage == 1:
                def chunk(k, middle=middle):
                    return middle[pl.ds(k, 1)][0]
            elif axis == "y":
                def chunk(k, window=window):
                    return part[pl.ds(k, 1), :, :, window][0]
            else:
                def chunk(k, window=window):
                    return part[:, pl.ds(k, 1), :, window][:, 0]

            messages = stage_messages(kind, n, long)
            names = [(index, stage, name, step) for name, step, _, _ in messages]
            slot_of = {name: slot for slot, name in enumerate(names)}

            def put(key, value, device, slot_of=slot_of, send_buf=send_buf, recv_buf=recv_buf, sem=sem):
                slot = slot_of[key]
                send_buf[slot] = value.astype(BF16)
                copies[key] = send(
                    send_buf.at[slot], recv_buf.at[slot], rs_send.at[sem + slot], rs_recv.at[sem + slot], device
                )

            def got(key, slot_of=slot_of, recv_buf=recv_buf):
                copies[key].wait_recv()
                return recv_buf[slot_of[key]].astype(F32)

            def total(keys, at=at, chunk=chunk, got=got, stage=stage, middle=middle, first=first, cols=cols):
                value = chunk(at(0))
                for key in keys:
                    value = value + got(key)
                if stage == 0:
                    middle[...] = value
                else:
                    final[:, first:first + cols] = value

            if kind == "ring":
                for key, (name, step, way, _) in zip(names, messages):
                    last = n // 2 if name == "far" else n // 2 - 1

                    def forward(
                        key=key, step=step, way=way, last=last, at=at, dev=dev, chunk=chunk, got=got, put=put
                    ):
                        value = chunk(at(way * (last - step + 1)))
                        if step > 1:
                            value = value + got(key[:3] + (step - 1,))
                        put(key, value, dev(way))

                    steps[key] = forward
                ends = [key for key in names if key[3] == (n // 2 if key[2] == "far" else n // 2 - 1)]
            else:
                def spread(names=names, at=at, dev=dev, chunk=chunk, put=put):
                    for key in names:
                        put(key, chunk(at(key[3])), dev(key[3]))

                steps[index, stage, "all"] = spread
                ends = names
            steps[index, stage, "sum"] = functools.partial(total, ends)
            sem += n - 1

    for key in schedule(sizes, slots):
        steps[key]()

    base = cent_unit[pl.ds(pl.multiple_of(pts * share, share), share), :].astype(F32)
    out_ref[...] = unit_rms(base + 8.0 * final[...]).astype(BF16)
    for copy in pending:
        copy.wait_send()


def local(mesh_pts, mesh_own, points, parent_of, owner_of, child_count, centroids):
    ny = NY
    nz = mesh_pts // ny
    nx = mesh_own // CORES
    tokens, width = points.shape
    slots = centroids.shape[1]
    parents = owner_of.shape[0]
    share = slots // mesh_pts
    groups = mesh_own
    tile_shapes = []
    sems = 0
    for order, _, cols, _, _ in TILES:
        n1, n2 = (ny, nz) if order == "yz" else (nz, ny)
        tile_shapes += [
            pltpu.VMEM((n1 - 1, n2, share, cols), BF16),
            pltpu.VMEM((n1 - 1, n2, share, cols), BF16),
            pltpu.VMEM((n2, share, cols), F32),
            pltpu.VMEM((n2 - 1, share, cols), BF16),
            pltpu.VMEM((n2 - 1, share, cols), BF16),
        ]
        sems += n1 + n2 - 2
    dma = pltpu.SemaphoreType.DMA
    out = pl.pallas_call(
        functools.partial(kernel_entry, ny, nz, nx, len(tile_shapes)),
        out_shape=jax.ShapeDtypeStruct((share, width), BF16),
        in_specs=[pl.BlockSpec(memory_space=pl.ANY)]
        + [pl.BlockSpec(memory_space=pltpu.VMEM)] * 3
        + [pl.BlockSpec(memory_space=pl.ANY)],
        out_specs=pl.BlockSpec(memory_space=pltpu.VMEM),
        scratch_shapes=[
            pltpu.VMEM((tokens, width), BF16),
            pltpu.VMEM((slots, width), BF16),
            pltpu.VMEM((slots, width), BF16),
            pltpu.VMEM((tokens, width), BF16),
            pltpu.VMEM((nx * PAIR, width), BF16),
            pltpu.VMEM((groups * CAP, width), BF16),
            pltpu.VMEM((parents, slots), BF16),
            pltpu.VMEM((groups * CAP, parents), BF16),
            pltpu.VMEM((groups, tokens), F32),
            pltpu.VMEM((groups * CAP, slots), F32),
            pltpu.VMEM((slots, groups * CAP), BF16),
            pltpu.VMEM((ny, nz, share, width), F32),
            pltpu.VMEM((share, width), F32),
            pltpu.VMEM((SWEEPS, 1, slots), F32),
            pltpu.VMEM((SWEEPS, ny * nz - 1, 1, slots), F32),
            *tile_shapes,
            dma,
            dma,
            dma((groups,)),
            dma((groups,)),
            dma((groups,)),
            dma((groups,)),
            dma((groups,)),
            dma((groups,)),
            dma((SWEEPS, ny * nz - 1)),
            dma((SWEEPS, ny * nz - 1)),
            dma((sems,)),
            dma((sems,)),
            pltpu.SemaphoreType.REGULAR((3,)),
        ],
        compiler_params=pltpu.CompilerParams(
            collective_id=0, has_side_effects=True, vmem_limit_bytes=60 * 1024 * 1024
        ),
    )(
        points,
        parent_of.reshape(1, groups * tokens),
        owner_of.reshape(1, parents),
        child_count.reshape(1, parents),
        centroids[0],
    )
    return out[None]


def kernel_entry(ny, nz, nx, tiles, *refs):
    head, rest = refs[:6 + 15], refs[6 + 15:]
    return kernel(ny, nz, nx, *head, rest[:tiles], *rest[tiles:])


def solution(mesh):
    in_specs = (P(("pts", "own"), None), P("pts", None), P(), P(), P("own", None, None))
    out_specs = P("own", "pts", None)
    body = functools.partial(local, mesh.shape["pts"], mesh.shape["own"])
    return jax.shard_map(body, mesh=mesh, in_specs=in_specs, out_specs=out_specs, check_vma=False)
```

```python
import functools

import jax
import jax.numpy as jnp
from jax import lax
from jax.experimental import pallas as pl
from jax.experimental.pallas import tpu as pltpu
from jax.sharding import PartitionSpec as P

SWEEPS = 2
CAP = 64
PAIR = 96
HALF = PAIR // 2
EXTRA = CAP - HALF
LAST = 384
CORES = 2
NY = 4
MESH = pl.DeviceIdType.MESH
F32 = jnp.float32
BF16 = jnp.bfloat16

GROUP = 256
TILES = (
    ("yz", 0, 256, -1, "direct", 0),
    ("zy", 1, 128, 1, "direct", 0),
    ("zy", 1, 128, -1, "direct", 0),
    ("zy", 2, 128, -1, "direct", 0),
    ("zy", 2, 128, 1, "direct", 0),
    ("yz", 3, 256, 1, "direct", 0),
    ("yz", 4, 128, -1, "ring", 0),
    ("yz", 4, 128, 1, "ring", 0),
    ("zy", 5, 128, -1, "direct", 0),
    ("zy", 5, 128, 1, "direct", 0),
)


def stage_messages(mode, n, long):
    far = n // 2
    if mode == "ring":
        return [("far", t, long, 1) for t in range(1, far + 1)] + [("near", t, -long, 1) for t in range(1, far)]
    return [("one", long * far, long, far)] + [
        ("one", hops * way, way, hops) for hops in range(far - 1, 0, -1) for way in (long, -long)
    ]


def tile_tasks(index, tile, sizes, slots):
    order, group, cols, long, mode, _ = tile
    share = slots
    for axis in order:
        share //= sizes[axis]
    before = ("product", group)
    tasks = {before: ((), (), 0.69, ())}
    for stage, axis in enumerate(order):
        n = sizes[axis]
        chunk = (slots // n if stage == 0 else share) * cols
        work = chunk * 1.526e-6
        kind = "ring" if stage == 0 else mode
        messages = stage_messages(kind, n, long)
        names = [(index, stage, name, step) for name, step, _, _ in messages]
        wire = [(name, axis, way, hops, chunk * 2) for name, (_, _, way, hops) in zip(names, messages)]
        done = (index, stage, "sum")
        if kind == "ring":
            for key, one in zip(names, wire):
                last = key[:3] + (key[3] - 1,)
                first = key[3] == 1
                tasks[key] = ((before,) if first else (last,), () if first else (last,), work + 0.03, (one,))
            ends = [(index, stage, "far", n // 2)] + ([(index, stage, "near", n // 2 - 1)] if n > 2 else [])
            tasks[done] = (tuple(ends), tuple(ends), 2 * work + 0.03, ())
        else:
            tasks[index, stage, "all"] = ((before,), (), n * work + 0.03, tuple(wire))
            tasks[done] = (((index, stage, "all"),), tuple(names), n * work + 0.03, ())
        before = done
    return tasks


def schedule(sizes, slots):
    rate, hop_us, next_hop_us = 46500.0, 1.5, 0.75
    tasks = {}
    for index, tile in enumerate(TILES):
        tasks.update(tile_tasks(index, tile, sizes, slots))
    sender = {message[0]: key for key, task in tasks.items() for message in task[3]}
    after = {key: [] for key in tasks}
    for key, (before, waits, _, _) in tasks.items():
        for one in before:
            after[one].append((key, 0.0))
        for one in waits:
            after[sender[one]].append((key, hop_us))
    chain = {}

    def length(key):
        if key not in chain:
            chain[key] = tasks[key][2] + max([gap + length(one) for one, gap in after[key]], default=0.0)
        return chain[key]

    def rank(key):
        heads = [one[0] for one, _ in after[key]] if key[0] == "product" else [key[0]]
        return length(key) + max(TILES[index][5] for index in heads)

    now, order, arrival, link_free, done = 0.0, [], {}, {}, set()
    while len(order) < len(tasks):
        ready = []
        for key, (before, waits, _, _) in tasks.items():
            if key not in done and all(one in done for one in before) and all(one in arrival for one in waits):
                ready.append((max([arrival[one] for one in waits], default=0.0), key))
        started = [one for one in ready if one[0] <= now]
        if started:
            at, key = max(started, key=lambda one: rank(one[1]))
        else:
            at, key = min(ready, key=lambda one: (one[0], -rank(one[1])))
        now = max(now, at) + tasks[key][2]
        for name, axis, way, hops, size in tasks[key][3]:
            start = max(now, link_free.get((axis, way), 0.0))
            link_free[axis, way] = start + hops * size / rate
            arrival[name] = link_free[axis, way] + hop_us + next_hop_us * (hops - 1)
        done.add(key)
        order.append(key)
    return order


def unit_rms(values):
    values = values.astype(F32)
    return values * lax.rsqrt(jnp.mean(values * values, axis=-1, keepdims=True) + 1e-06)


def iota(shape, dim):
    return lax.broadcasted_iota(jnp.int32, shape, dim).astype(F32)


def kernel(
    ny, nz, nx,
    points_hbm, parent_hbm, owner_hbm, count_hbm, cent_hbm, out_ref,
    parent_ref, owner_ref, count_ref, point_raw, cent_raw, cent_unit, point_unit, packed, rows, member, onehot, place, weights, assign_t, part, final,
    sum_send, sum_recv, tile_bufs,
    small_sem, point_sem, cent_sem, x_send, x_recv, l_send, l_recv, f_send, f_recv, s_send, s_recv, rs_send, rs_recv,
    round_sem,
):
    pts, me = lax.axis_index("pts"), lax.axis_index("own")
    y, z = lax.div(pts, nz), lax.rem(pts, nz)
    x, core = lax.div(me, CORES), lax.rem(me, CORES)
    groups = nx * CORES
    tokens, width = points_hbm.shape
    parents = owner_hbm.shape[1]
    slots = cent_hbm.shape[0]

    def own_at(dx, dc, sign):
        other = lax.rem(x + (dx if sign > 0 else nx - dx), nx)
        return other * CORES + (core if dc == 0 else 1 - core)

    def at_y(step):
        return lax.rem(y + step + ny, ny)

    def at_z(step):
        return lax.rem(z + step + nz, nz)

    def dev_y(step):
        return (at_y(step) * nz + z, me)

    def dev_z(step):
        return (y * nz + at_z(step), me)

    offsets = [(dx, dc) for dx in range(nx) for dc in range(CORES)]
    barrier = pltpu.get_barrier_semaphore()
    peers = [(pts, own_at(dx, dc, 1)) for dx, dc in offsets if (dx, dc) != (0, 0)]
    peers += [dev_y(s) for s in range(1, ny)] + [dev_z(1), dev_z(-1)]
    for peer in peers:
        pl.semaphore_signal(barrier, inc=1, device_id=peer, device_id_type=MESH)
    small = [
        pltpu.make_async_copy(source, target, small_sem.at[i])
        for i, (source, target) in enumerate(
            ((owner_hbm, owner_ref), (count_hbm, count_ref), (parent_hbm, parent_ref))
        )
    ]
    for copy in small:
        copy.start()
    point_copy = pltpu.make_async_copy(points_hbm, point_raw, point_sem)
    point_copy.start()
    cent_copy = pltpu.make_async_copy(cent_hbm, cent_raw, cent_sem)
    cent_copy.start()

    pending = []

    def send(src, dst, send_sem, recv_sem, device):
        copy = pltpu.make_async_remote_copy(
            src_ref=src, dst_ref=dst, send_sem=send_sem, recv_sem=recv_sem,
            device_id=device, device_id_type=MESH,
        )
        copy.start()
        pending.append(copy)
        return copy

    for copy in small:
        copy.wait()

    square = (parents, parents)
    owner_row = owner_ref[...].astype(F32)
    count_row = count_ref[...].astype(F32)
    diagonal = iota(square, 0) == iota(square, 1)
    owner_col = jnp.sum(jnp.where(diagonal, owner_row, 0.0), axis=1, keepdims=True)
    count_col = jnp.sum(jnp.where(diagonal, count_row, 0.0), axis=1, keepdims=True)
    upper = jnp.where(iota((tokens, tokens), 0) <= iota((tokens, tokens), 1), 1.0, 0.0).astype(BF16)
    parent_iota = iota((parents, tokens), 0)

    def owners_of_block(index):
        parent = parent_ref[:, pl.ds(pl.multiple_of(index * tokens, tokens), tokens)].astype(F32)
        return parent, jnp.sum(jnp.where(parent_iota == parent, owner_col, 0.0), axis=0, keepdims=True)

    _, my_owner = owners_of_block(me)
    goes = my_owner == iota((groups, tokens), 0)
    rank = jnp.dot(jnp.where(goes, 1.0, 0.0).astype(BF16), upper, preferred_element_type=F32)
    odd = lax.rem(lax.broadcasted_iota(jnp.int32, (groups, tokens), 0), CORES) == 1
    place[...] = jnp.where(goes, jnp.where(odd, PAIR - rank, rank - 1.0), -1.0)
    point_copy.wait()
    point_unit[...] = unit_rms(point_raw[...]).astype(BF16)

    pair_iota = iota((PAIR, tokens), 0)
    near, far = (1, nx - 1), (nx // 2,)
    blocks = [(dx, dc) for dx in (0,) + far + near for dc in range(CORES)]
    block_of = {offset: i for i, offset in enumerate(blocks)}

    def pack(group):
        picks = []
        for dx in group:
            chip = lax.rem(x + dx, nx) * CORES
            taken = place[pl.ds(chip, 1), :] == pair_iota
            for other in range(1, CORES):
                taken = taken | (place[pl.ds(chip + other, 1), :] == pair_iota)
            picks.append(jnp.where(taken, 1.0, 0.0).astype(BF16))
        block = jnp.dot(jnp.concatenate(picks, axis=0), point_unit[...], preferred_element_type=F32).astype(BF16)
        for i, dx in enumerate(group):
            packed[dx * PAIR:(dx + 1) * PAIR, :] = block[i * PAIR:(i + 1) * PAIR]

    def part_of(start, size):
        return pl.ds(pl.multiple_of(start, EXTRA), size)

    arrivals, lasts, forwards = {}, {}, {}

    early, late = slice(0, width - LAST), slice(width - LAST, width)

    def depart(group):
        for window in (early, late):
            for dx in group:
                for dc in range(CORES):
                    k = block_of[dx, dc]
                    to_core = core if dc == 0 else 1 - core
                    device = (pts, own_at(dx, dc, 1))
                    span = slice(0, width) if group is far else window
                    if window is early:
                        arrivals[dx, dc] = send(
                            packed.at[part_of(dx * PAIR + HALF * to_core, HALF), span],
                            rows.at[part_of(k * CAP + EXTRA * to_core, HALF), span],
                            x_send.at[k], x_recv.at[k], device,
                        )
                    elif group is near:
                        lasts[dx, dc] = send(
                            packed.at[part_of(dx * PAIR + (PAIR - CAP) * to_core, CAP), span],
                            rows.at[pl.ds(k * CAP, CAP), span],
                            l_send.at[k], l_recv.at[k], device,
                        )

    def hand_over(group, span):
        for dx in group:
            for dc in range(CORES):
                k, other = block_of[dx, dc], block_of[dx, 1 - dc]
                arrivals[dx, dc].wait_recv()
                forwards[dx, dc] = send(
                    rows.at[part_of(k * CAP + 2 * EXTRA - EXTRA * core, EXTRA), span],
                    rows.at[part_of(other * CAP + HALF * core, EXTRA), span],
                    f_send.at[k], f_recv.at[other], (pts, own_at(0, 1, 1)),
                )

    def handed_over(group):
        for dx in group:
            for dc in range(CORES):
                forwards[dx, dc].wait_recv()

    pack(far)
    pl.semaphore_wait(barrier, len(peers))
    for step in (1, -1):
        pl.semaphore_signal(round_sem.at[0], inc=1, device_id=dev_z(step), device_id_type=MESH)
    depart(far)
    pack(near)
    depart(near)
    pack((0,))
    mine, theirs = block_of[0, 0], block_of[0, 1]
    rows[mine * CAP:(mine + 1) * CAP, :] = packed[part_of((PAIR - CAP) * core, CAP), :]
    arrivals[0, 1] = send(
        packed.at[part_of((PAIR - CAP) * (1 - core), CAP)], rows.at[pl.ds(theirs * CAP, CAP)],
        x_send.at[theirs], x_recv.at[theirs], (pts, own_at(0, 1, 1)),
    )

    first_col = jnp.sum(
        jnp.where((owner_col == owner_row) & (iota(square, 1) < iota(square, 0)), count_row, 0.0),
        axis=1, keepdims=True,
    )
    my_index = me.astype(F32)
    slot_row = iota((parents, slots), 1)
    member[...] = jnp.where(
        (owner_col == my_index) & (slot_row >= first_col) & (slot_row < first_col + count_col), 1.0, 0.0
    ).astype(BF16)
    block_parent, block_live = [], []
    for dx, dc in blocks:
        parent, owner = owners_of_block(own_at(dx, dc, -1))
        block_parent.append(parent)
        block_live.append(owner == my_index)
    live = jnp.concatenate([jnp.where(one, 1.0, 0.0) for one in block_live], axis=0)
    rank = jnp.dot(live.astype(BF16), upper, preferred_element_type=F32)
    spot = jnp.where(live > 0.5, rank - 1.0, -1.0)
    slot_iota = iota((CAP, tokens), 0)
    slot_iota = jnp.where(core == 0, slot_iota, (CAP - 1.0) - slot_iota)
    for k in range(groups):
        chosen = spot[k:k + 1, :] == slot_iota
        parent = jnp.sum(jnp.where(chosen, block_parent[k] + 1.0, 0.0), axis=1, keepdims=True) - 1.0
        onehot[k * CAP:(k + 1) * CAP, :] = jnp.where(parent == iota((CAP, parents), 1), 1.0, 0.0).astype(BF16)

    cent_copy.wait()
    step_rows = 64

    @pl.loop(0, slots // step_rows)
    def _(i):
        span = pl.ds(pl.multiple_of(i * step_rows, step_rows), step_rows)
        cent_unit[span, :] = unit_rms(cent_raw[span, :]).astype(BF16)

    pl.semaphore_wait(round_sem.at[0], 2)
    for step in (2, -2):
        pl.semaphore_signal(round_sem.at[1], inc=1, device_id=dev_z(step), device_id_type=MESH)

    scale = 1.0 / (width * 0.05)
    wide = 256

    def score(span, cols, depth):
        return lax.dot_general(
            rows[span, depth], cent_unit[cols, depth], (((1,), (1,)), ((), ())), preferred_element_type=F32
        )

    def weigh(span, cols, value):
        allowed = jnp.dot(onehot[span, :], member[:, cols], preferred_element_type=F32)
        value = jnp.where(allowed > 0.5, jnp.exp(value * scale), 0.0)
        weights[span, cols] = value
        return jnp.sum(value, axis=0, keepdims=True)

    first_rows = (1 + len(far)) * CORES * CAP
    top, bottom = slice(0, first_rows), slice(first_rows, groups * CAP)
    slot_cols = [slice(n * wide, (n + 1) * wide) for n in range(slots // wide)]
    arrivals[0, 1].wait_recv()
    hand_over(far, slice(0, width))
    handed_over(far)
    sums = [weigh(top, cols, score(top, cols, slice(0, width))) for cols in slot_cols]
    pl.semaphore_wait(round_sem.at[1], 2)
    for step in (1, -1):
        pl.semaphore_signal(round_sem.at[2], inc=1, device_id=dev_z(step), device_id_type=MESH)
    hand_over(near, early)
    handed_over(near)
    for cols in slot_cols:
        weights[bottom, cols] = score(bottom, cols, early)
    for dx in near:
        for dc in range(CORES):
            lasts[dx, dc].wait_recv()
    for n, cols in enumerate(slot_cols):
        sums[n] = sums[n] + weigh(bottom, cols, weights[bottom, cols] + score(bottom, cols, late))
    column = jnp.concatenate(sums, axis=1)
    pl.semaphore_wait(round_sem.at[2], 2)

    plane = sorted(
        ((dy, dz) for dy in range(ny) for dz in range(nz) if (dy, dz) != (0, 0)),
        key=lambda one: -min(one[0], ny - one[0]) - min(one[1], nz - one[1]),
    )

    def column_total(sweep, local):
        sum_send[sweep] = local
        copies = [
            send(sum_send.at[sweep], sum_recv.at[sweep, k], s_send.at[sweep, k], s_recv.at[sweep, k],
                 (at_y(dy) * nz + at_z(dz), me))
            for k, (dy, dz) in enumerate(plane)
        ]
        total = local
        for k, copy in reversed(list(enumerate(copies))):
            copy.wait_recv()
            total = total + sum_recv[sweep, k]
        return total

    row_step = 128
    for sweep in range(SWEEPS):
        total = column_total(sweep, column)
        inverse = 1.0 / jnp.where(total > 0.0, total, 1.0)
        column = None
        for i in range(groups * CAP // row_step):
            span = slice(i * row_step, (i + 1) * row_step)
            value = weights[span, :] * inverse
            row_sum = jnp.sum(value, axis=1, keepdims=True)
            value = value * (1.0 / jnp.where(row_sum > 0.0, row_sum, 1.0))
            if sweep < SWEEPS - 1:
                weights[span, :] = value
                partial = jnp.sum(value, axis=0, keepdims=True)
                column = partial if column is None else column + partial
            else:
                assign_t[:, span] = jnp.transpose(value).astype(BF16)

    share = slots // (ny * nz)
    sizes = {"y": ny, "z": nz}
    places = {"y": (at_y, dev_y), "z": (at_z, dev_z)}
    steps, copies = {}, {}
    sem = 0
    taken_columns = [group * GROUP for group in range(width // GROUP)]
    for group in {tile[1] for tile in TILES}:
        def product(span=slice(group * GROUP, (group + 1) * GROUP)):
            value = jnp.dot(assign_t[...], rows[:, span], preferred_element_type=F32)
            part[:, :, :, span] = value.reshape(ny, nz, share, GROUP)

        steps["product", group] = product
    for index, (order, group_of, cols, long, mode, _) in enumerate(TILES):
        send1, recv1, middle, send2, recv2 = tile_bufs[5 * index:5 * index + 5]
        first = taken_columns[group_of]
        taken_columns[group_of] += cols
        window = pl.ds(first, cols)

        for stage, axis in enumerate(order):
            n = sizes[axis]
            at, dev = places[axis]
            kind = "ring" if stage == 0 else mode
            send_buf, recv_buf = (send1, recv1) if stage == 0 else (send2, recv2)
            if stage == 1:
                def chunk(k, middle=middle):
                    return middle[pl.ds(k, 1)][0]
            elif axis == "y":
                def chunk(k, window=window):
                    return part[pl.ds(k, 1), :, :, window][0]
            else:
                def chunk(k, window=window):
                    return part[:, pl.ds(k, 1), :, window][:, 0]

            messages = stage_messages(kind, n, long)
            names = [(index, stage, name, step) for name, step, _, _ in messages]
            slot_of = {name: slot for slot, name in enumerate(names)}

            def put(key, value, device, slot_of=slot_of, send_buf=send_buf, recv_buf=recv_buf, sem=sem):
                slot = slot_of[key]
                send_buf[slot] = value.astype(BF16)
                copies[key] = send(
                    send_buf.at[slot], recv_buf.at[slot], rs_send.at[sem + slot], rs_recv.at[sem + slot], device
                )

            def got(key, slot_of=slot_of, recv_buf=recv_buf):
                copies[key].wait_recv()
                return recv_buf[slot_of[key]].astype(F32)

            def total(keys, at=at, chunk=chunk, got=got, stage=stage, middle=middle, first=first, cols=cols):
                value = chunk(at(0))
                for key in keys:
                    value = value + got(key)
                if stage == 0:
                    middle[...] = value
                else:
                    final[:, first:first + cols] = value

            if kind == "ring":
                for key, (name, step, way, _) in zip(names, messages):
                    last = n // 2 if name == "far" else n // 2 - 1

                    def forward(
                        key=key, step=step, way=way, last=last, at=at, dev=dev, chunk=chunk, got=got, put=put
                    ):
                        value = chunk(at(way * (last - step + 1)))
                        if step > 1:
                            value = value + got(key[:3] + (step - 1,))
                        put(key, value, dev(way))

                    steps[key] = forward
                ends = [key for key in names if key[3] == (n // 2 if key[2] == "far" else n // 2 - 1)]
            else:
                def spread(names=names, at=at, dev=dev, chunk=chunk, put=put):
                    for key in names:
                        put(key, chunk(at(key[3])), dev(key[3]))

                steps[index, stage, "all"] = spread
                ends = names
            steps[index, stage, "sum"] = functools.partial(total, ends)
            sem += n - 1

    for key in schedule(sizes, slots):
        steps[key]()

    base = cent_unit[pl.ds(pl.multiple_of(pts * share, share), share), :].astype(F32)
    out_ref[...] = unit_rms(base + 8.0 * final[...]).astype(BF16)
    for copy in pending:
        copy.wait_send()


def local(mesh_pts, mesh_own, points, parent_of, owner_of, child_count, centroids):
    ny = NY
    nz = mesh_pts // ny
    nx = mesh_own // CORES
    tokens, width = points.shape
    slots = centroids.shape[1]
    parents = owner_of.shape[0]
    share = slots // mesh_pts
    groups = mesh_own
    tile_shapes = []
    sems = 0
    for order, _, cols, _, _, _ in TILES:
        n1, n2 = (ny, nz) if order == "yz" else (nz, ny)
        tile_shapes += [
            pltpu.VMEM((n1 - 1, n2, share, cols), BF16),
            pltpu.VMEM((n1 - 1, n2, share, cols), BF16),
            pltpu.VMEM((n2, share, cols), F32),
            pltpu.VMEM((n2 - 1, share, cols), BF16),
            pltpu.VMEM((n2 - 1, share, cols), BF16),
        ]
        sems += n1 + n2 - 2
    dma = pltpu.SemaphoreType.DMA
    operands = (
        points,
        parent_of.reshape(1, groups * tokens),
        owner_of.reshape(1, parents),
        child_count.reshape(1, parents),
        centroids[0],
    )
    out = pl.pallas_call(
        functools.partial(kernel_entry, ny, nz, nx, len(tile_shapes)),
        out_shape=jax.ShapeDtypeStruct((share, width), BF16),
        in_specs=[pl.BlockSpec(memory_space=pl.ANY)] * 5,
        out_specs=pl.BlockSpec(memory_space=pltpu.VMEM),
        scratch_shapes=[
            pltpu.VMEM((1, groups * tokens), jnp.int32),
            pltpu.VMEM((1, parents), jnp.int32),
            pltpu.VMEM((1, parents), jnp.int32),
            pltpu.VMEM((tokens, width), BF16),
            pltpu.VMEM((slots, width), BF16),
            pltpu.VMEM((slots, width), BF16),
            pltpu.VMEM((tokens, width), BF16),
            pltpu.VMEM((nx * PAIR, width), BF16),
            pltpu.VMEM((groups * CAP, width), BF16),
            pltpu.VMEM((parents, slots), BF16),
            pltpu.VMEM((groups * CAP, parents), BF16),
            pltpu.VMEM((groups, tokens), F32),
            pltpu.VMEM((groups * CAP, slots), F32),
            pltpu.VMEM((slots, groups * CAP), BF16),
            pltpu.VMEM((ny, nz, share, width), F32),
            pltpu.VMEM((share, width), F32),
            pltpu.VMEM((SWEEPS, 1, slots), F32),
            pltpu.VMEM((SWEEPS, ny * nz - 1, 1, slots), F32),
            *tile_shapes,
            dma((3,)),
            dma,
            dma,
            dma((groups,)),
            dma((groups,)),
            dma((groups,)),
            dma((groups,)),
            dma((groups,)),
            dma((groups,)),
            dma((SWEEPS, ny * nz - 1)),
            dma((SWEEPS, ny * nz - 1)),
            dma((sems,)),
            dma((sems,)),
            pltpu.SemaphoreType.REGULAR((3,)),
        ],
        compiler_params=pltpu.CompilerParams(
            collective_id=0, has_side_effects=True, vmem_limit_bytes=36 * 1024 * 1024
        ),
    )(
        *(pltpu.with_memory_space_constraint(one, pltpu.HBM) for one in operands)
    )
    return out[None]


def kernel_entry(ny, nz, nx, tiles, *refs):
    head, rest = refs[:6 + 18], refs[6 + 18:]
    return kernel(ny, nz, nx, *head, rest[:tiles], *rest[tiles:])


def solution(mesh):
    in_specs = (P(("pts", "own"), None), P("pts", None), P(), P(), P("own", None, None))
    out_specs = P("own", "pts", None)
    body = functools.partial(local, mesh.shape["pts"], mesh.shape["own"])
    return jax.shard_map(body, mesh=mesh, in_specs=in_specs, out_specs=out_specs, check_vma=False)
```

```python
import functools

import jax
import jax.numpy as jnp
from jax import lax
from jax.experimental import pallas as pl
from jax.experimental.pallas import tpu as pltpu
from jax.sharding import PartitionSpec as P

SWEEPS = 2
CAP = 64
PAIR = 96
HALF = PAIR // 2
EXTRA = CAP - HALF
LAST = 384
NEVER = -1e30
CORES = 2
NY = 4
MESH = pl.DeviceIdType.MESH
F32 = jnp.float32
BF16 = jnp.bfloat16

GROUP = 256
TILES = (
    ("yz", 0, 256, -1, "direct", 0),
    ("zy", 1, 128, 1, "direct", 0),
    ("zy", 1, 128, -1, "direct", 0),
    ("zy", 2, 128, -1, "direct", 0),
    ("zy", 2, 128, 1, "direct", 0),
    ("yz", 3, 256, 1, "direct", 0),
    ("yz", 4, 128, -1, "ring", 0),
    ("yz", 4, 128, 1, "ring", 0),
    ("zy", 5, 128, -1, "direct", 0),
    ("zy", 5, 128, 1, "direct", 0),
)


def stage_messages(mode, n, long):
    far = n // 2
    if mode == "ring":
        return [("far", t, long, 1) for t in range(1, far + 1)] + [("near", t, -long, 1) for t in range(1, far)]
    return [("one", long * far, long, far)] + [
        ("one", hops * way, way, hops) for hops in range(far - 1, 0, -1) for way in (long, -long)
    ]


def tile_tasks(index, tile, sizes, slots):
    order, group, cols, long, mode, _ = tile
    share = slots
    for axis in order:
        share //= sizes[axis]
    before = ("product", group)
    tasks = {before: ((), (), 0.69, ())}
    for stage, axis in enumerate(order):
        n = sizes[axis]
        chunk = (slots // n if stage == 0 else share) * cols
        work = chunk * 1.526e-6
        kind = "ring" if stage == 0 else mode
        messages = stage_messages(kind, n, long)
        names = [(index, stage, name, step) for name, step, _, _ in messages]
        wire = [(name, axis, way, hops, chunk * 2) for name, (_, _, way, hops) in zip(names, messages)]
        done = (index, stage, "sum")
        if kind == "ring":
            for key, one in zip(names, wire):
                last = key[:3] + (key[3] - 1,)
                first = key[3] == 1
                tasks[key] = ((before,) if first else (last,), () if first else (last,), work + 0.03, (one,))
            ends = [(index, stage, "far", n // 2)] + ([(index, stage, "near", n // 2 - 1)] if n > 2 else [])
            tasks[done] = (tuple(ends), tuple(ends), 2 * work + 0.03, ())
        else:
            tasks[index, stage, "all"] = ((before,), (), n * work + 0.03, tuple(wire))
            tasks[done] = (((index, stage, "all"),), tuple(names), n * work + 0.03, ())
        before = done
    return tasks


def schedule(sizes, slots):
    rate, hop_us, next_hop_us = 46500.0, 1.5, 0.75
    tasks = {}
    for index, tile in enumerate(TILES):
        tasks.update(tile_tasks(index, tile, sizes, slots))
    sender = {message[0]: key for key, task in tasks.items() for message in task[3]}
    after = {key: [] for key in tasks}
    for key, (before, waits, _, _) in tasks.items():
        for one in before:
            after[one].append((key, 0.0))
        for one in waits:
            after[sender[one]].append((key, hop_us))
    chain = {}

    def length(key):
        if key not in chain:
            chain[key] = tasks[key][2] + max([gap + length(one) for one, gap in after[key]], default=0.0)
        return chain[key]

    def rank(key):
        heads = [one[0] for one, _ in after[key]] if key[0] == "product" else [key[0]]
        return length(key) + max(TILES[index][5] for index in heads)

    now, order, arrival, link_free, done = 0.0, [], {}, {}, set()
    while len(order) < len(tasks):
        ready = []
        for key, (before, waits, _, _) in tasks.items():
            if key not in done and all(one in done for one in before) and all(one in arrival for one in waits):
                ready.append((max([arrival[one] for one in waits], default=0.0), key))
        started = [one for one in ready if one[0] <= now]
        if started:
            at, key = max(started, key=lambda one: rank(one[1]))
        else:
            at, key = min(ready, key=lambda one: (one[0], -rank(one[1])))
        now = max(now, at) + tasks[key][2]
        for name, axis, way, hops, size in tasks[key][3]:
            start = max(now, link_free.get((axis, way), 0.0))
            link_free[axis, way] = start + hops * size / rate
            arrival[name] = link_free[axis, way] + hop_us + next_hop_us * (hops - 1)
        done.add(key)
        order.append(key)
    return order


def unit_rms(values):
    values = values.astype(F32)
    return values * lax.rsqrt(jnp.mean(values * values, axis=-1, keepdims=True) + 1e-06)


def iota(shape, dim):
    return lax.broadcasted_iota(jnp.int32, shape, dim).astype(F32)


def kernel(
    ny, nz, nx,
    points_hbm, parent_hbm, owner_hbm, count_hbm, cent_hbm, out_ref,
    parent_ref, owner_ref, count_ref, point_raw, cent_raw, cent_unit, point_unit, packed, rows, member, onehot, place, weights, assign_t, part, final,
    sum_send, sum_recv, tile_bufs,
    small_sem, point_sem, cent_sem, x_send, x_recv, l_send, l_recv, f_send, f_recv, s_send, s_recv, rs_send, rs_recv,
    round_sem,
):
    pts, me = lax.axis_index("pts"), lax.axis_index("own")
    y, z = lax.div(pts, nz), lax.rem(pts, nz)
    x, core = lax.div(me, CORES), lax.rem(me, CORES)
    groups = nx * CORES
    tokens, width = points_hbm.shape
    parents = owner_hbm.shape[1]
    slots = cent_hbm.shape[0]

    def own_at(dx, dc, sign):
        other = lax.rem(x + (dx if sign > 0 else nx - dx), nx)
        return other * CORES + (core if dc == 0 else 1 - core)

    def at_y(step):
        return lax.rem(y + step + ny, ny)

    def at_z(step):
        return lax.rem(z + step + nz, nz)

    def dev_y(step):
        return (at_y(step) * nz + z, me)

    def dev_z(step):
        return (y * nz + at_z(step), me)

    offsets = [(dx, dc) for dx in range(nx) for dc in range(CORES)]
    barrier = pltpu.get_barrier_semaphore()
    peers = [(pts, own_at(dx, dc, 1)) for dx, dc in offsets if (dx, dc) != (0, 0)]
    peers += [dev_y(s) for s in range(1, ny)] + [dev_z(1), dev_z(-1)]
    for peer in peers:
        pl.semaphore_signal(barrier, inc=1, device_id=peer, device_id_type=MESH)
    small = [
        pltpu.make_async_copy(source, target, small_sem.at[i])
        for i, (source, target) in enumerate(
            ((owner_hbm, owner_ref), (count_hbm, count_ref), (parent_hbm, parent_ref))
        )
    ]
    for copy in small:
        copy.start()
    point_copy = pltpu.make_async_copy(points_hbm, point_raw, point_sem)
    point_copy.start()
    cent_copy = pltpu.make_async_copy(cent_hbm, cent_raw, cent_sem)
    cent_copy.start()

    pending = []

    def send(src, dst, send_sem, recv_sem, device):
        copy = pltpu.make_async_remote_copy(
            src_ref=src, dst_ref=dst, send_sem=send_sem, recv_sem=recv_sem,
            device_id=device, device_id_type=MESH,
        )
        copy.start()
        pending.append(copy)
        return copy

    for copy in small:
        copy.wait()

    square = (parents, parents)
    owner_row = owner_ref[...].astype(F32)
    count_row = count_ref[...].astype(F32)
    diagonal = iota(square, 0) == iota(square, 1)
    owner_col = jnp.sum(jnp.where(diagonal, owner_row, 0.0), axis=1, keepdims=True)
    count_col = jnp.sum(jnp.where(diagonal, count_row, 0.0), axis=1, keepdims=True)
    upper = jnp.where(iota((tokens, tokens), 0) <= iota((tokens, tokens), 1), 1.0, 0.0).astype(BF16)
    parent_iota = iota((parents, tokens), 0)

    def owners_of_block(index):
        parent = parent_ref[:, pl.ds(pl.multiple_of(index * tokens, tokens), tokens)].astype(F32)
        return parent, jnp.sum(jnp.where(parent_iota == parent, owner_col, 0.0), axis=0, keepdims=True)

    _, my_owner = owners_of_block(me)
    goes = my_owner == iota((groups, tokens), 0)
    rank = jnp.dot(jnp.where(goes, 1.0, 0.0).astype(BF16), upper, preferred_element_type=F32)
    odd = lax.rem(lax.broadcasted_iota(jnp.int32, (groups, tokens), 0), CORES) == 1
    place[...] = jnp.where(goes, jnp.where(odd, PAIR - rank, rank - 1.0), -1.0)
    point_copy.wait()
    point_unit[...] = unit_rms(point_raw[...]).astype(BF16)

    pair_iota = iota((PAIR, tokens), 0)
    near, far = (1, nx - 1), (nx // 2,)
    blocks = [(dx, dc) for dx in (0,) + far + near for dc in range(CORES)]
    block_of = {offset: i for i, offset in enumerate(blocks)}

    def pack(group):
        picks = []
        for dx in group:
            chip = lax.rem(x + dx, nx) * CORES
            taken = place[pl.ds(chip, 1), :] == pair_iota
            for other in range(1, CORES):
                taken = taken | (place[pl.ds(chip + other, 1), :] == pair_iota)
            picks.append(jnp.where(taken, 1.0, 0.0).astype(BF16))
        block = jnp.dot(jnp.concatenate(picks, axis=0), point_unit[...], preferred_element_type=F32).astype(BF16)
        for i, dx in enumerate(group):
            packed[dx * PAIR:(dx + 1) * PAIR, :] = block[i * PAIR:(i + 1) * PAIR]

    def part_of(start, size):
        return pl.ds(pl.multiple_of(start, EXTRA), size)

    arrivals, lasts, forwards = {}, {}, {}

    early, late = slice(0, width - LAST), slice(width - LAST, width)

    def depart(group):
        for window in (early, late):
            for dx in group:
                for dc in range(CORES):
                    k = block_of[dx, dc]
                    to_core = core if dc == 0 else 1 - core
                    device = (pts, own_at(dx, dc, 1))
                    span = slice(0, width) if group is far else window
                    if window is early:
                        arrivals[dx, dc] = send(
                            packed.at[part_of(dx * PAIR + HALF * to_core, HALF), span],
                            rows.at[part_of(k * CAP + EXTRA * to_core, HALF), span],
                            x_send.at[k], x_recv.at[k], device,
                        )
                    elif group is near:
                        lasts[dx, dc] = send(
                            packed.at[part_of(dx * PAIR + (PAIR - CAP) * to_core, CAP), span],
                            rows.at[pl.ds(k * CAP, CAP), span],
                            l_send.at[k], l_recv.at[k], device,
                        )

    def hand_over(group, span):
        for dx in group:
            for dc in range(CORES):
                k, other = block_of[dx, dc], block_of[dx, 1 - dc]
                arrivals[dx, dc].wait_recv()
                forwards[dx, dc] = send(
                    rows.at[part_of(k * CAP + 2 * EXTRA - EXTRA * core, EXTRA), span],
                    rows.at[part_of(other * CAP + HALF * core, EXTRA), span],
                    f_send.at[k], f_recv.at[other], (pts, own_at(0, 1, 1)),
                )

    def handed_over(group):
        for dx in group:
            for dc in range(CORES):
                forwards[dx, dc].wait_recv()

    pack(far)
    pl.semaphore_wait(barrier, len(peers))
    for step in (1, -1):
        pl.semaphore_signal(round_sem.at[0], inc=1, device_id=dev_z(step), device_id_type=MESH)
    depart(far)
    pack(near)
    depart(near)
    pack((0,))
    mine, theirs = block_of[0, 0], block_of[0, 1]
    rows[mine * CAP:(mine + 1) * CAP, :] = packed[part_of((PAIR - CAP) * core, CAP), :]
    arrivals[0, 1] = send(
        packed.at[part_of((PAIR - CAP) * (1 - core), CAP)], rows.at[pl.ds(theirs * CAP, CAP)],
        x_send.at[theirs], x_recv.at[theirs], (pts, own_at(0, 1, 1)),
    )

    first_col = jnp.sum(
        jnp.where((owner_col == owner_row) & (iota(square, 1) < iota(square, 0)), count_row, 0.0),
        axis=1, keepdims=True,
    )
    my_index = me.astype(F32)
    slot_row = iota((parents, slots), 1)
    member[...] = jnp.where(
        (owner_col == my_index) & (slot_row >= first_col) & (slot_row < first_col + count_col), 1.0, 0.0
    ).astype(BF16)
    block_parent, block_live = [], []
    for dx, dc in blocks:
        parent, owner = owners_of_block(own_at(dx, dc, -1))
        block_parent.append(parent)
        block_live.append(owner == my_index)
    live = jnp.concatenate([jnp.where(one, 1.0, 0.0) for one in block_live], axis=0)
    rank = jnp.dot(live.astype(BF16), upper, preferred_element_type=F32)
    spot = jnp.where(live > 0.5, rank - 1.0, -1.0)
    slot_iota = iota((CAP, tokens), 0)
    slot_iota = jnp.where(core == 0, slot_iota, (CAP - 1.0) - slot_iota)
    for k in range(groups):
        chosen = spot[k:k + 1, :] == slot_iota
        parent = jnp.sum(jnp.where(chosen, block_parent[k] + 1.0, 0.0), axis=1, keepdims=True) - 1.0
        onehot[k * CAP:(k + 1) * CAP, :] = jnp.where(parent == iota((CAP, parents), 1), 1.0, 0.0).astype(BF16)

    cent_copy.wait()
    step_rows = 64

    @pl.loop(0, slots // step_rows)
    def _(i):
        span = pl.ds(pl.multiple_of(i * step_rows, step_rows), step_rows)
        cent_unit[span, :] = unit_rms(cent_raw[span, :]).astype(BF16)

    pl.semaphore_wait(round_sem.at[0], 2)
    for step in (2, -2):
        pl.semaphore_signal(round_sem.at[1], inc=1, device_id=dev_z(step), device_id_type=MESH)

    scale = 1.0 / (width * 0.05)
    wide = 256

    def score(span, cols, depth):
        return lax.dot_general(
            rows[span, depth], cent_unit[cols, depth], (((1,), (1,)), ((), ())), preferred_element_type=F32
        )

    def allowed(span, cols):
        return jnp.dot(onehot[span, :], member[:, cols], preferred_element_type=F32) > 0.5

    def weigh(span, cols, value):
        weights[span, cols] = value
        return jnp.sum(value, axis=0, keepdims=True)

    first_rows = (1 + len(far)) * CORES * CAP
    top, bottom = slice(0, first_rows), slice(first_rows, groups * CAP)
    slot_cols = [slice(n * wide, (n + 1) * wide) for n in range(slots // wide)]
    for cols in slot_cols:
        weights[bottom, cols] = jnp.where(allowed(bottom, cols), 0.0, NEVER)
    arrivals[0, 1].wait_recv()
    hand_over(far, slice(0, width))
    handed_over(far)
    sums = [
        weigh(top, cols, jnp.where(allowed(top, cols), jnp.exp(score(top, cols, slice(0, width)) * scale), 0.0))
        for cols in slot_cols
    ]
    pl.semaphore_wait(round_sem.at[1], 2)
    for step in (1, -1):
        pl.semaphore_signal(round_sem.at[2], inc=1, device_id=dev_z(step), device_id_type=MESH)
    hand_over(near, early)
    handed_over(near)
    for cols in slot_cols:
        weights[bottom, cols] += score(bottom, cols, early)
    for dx in near:
        for dc in range(CORES):
            lasts[dx, dc].wait_recv()
    for n, cols in enumerate(slot_cols):
        value = jnp.exp((weights[bottom, cols] + score(bottom, cols, late)) * scale)
        sums[n] = sums[n] + weigh(bottom, cols, value)
    column = jnp.concatenate(sums, axis=1)
    pl.semaphore_wait(round_sem.at[2], 2)

    plane = sorted(
        ((dy, dz) for dy in range(ny) for dz in range(nz) if (dy, dz) != (0, 0)),
        key=lambda one: -min(one[0], ny - one[0]) - min(one[1], nz - one[1]),
    )

    def column_total(sweep, local):
        sum_send[sweep] = local
        copies = [
            send(sum_send.at[sweep], sum_recv.at[sweep, k], s_send.at[sweep, k], s_recv.at[sweep, k],
                 (at_y(dy) * nz + at_z(dz), me))
            for k, (dy, dz) in enumerate(plane)
        ]
        total = local
        for k, copy in reversed(list(enumerate(copies))):
            copy.wait_recv()
            total = total + sum_recv[sweep, k]
        return total

    row_step = 128
    for sweep in range(SWEEPS):
        total = column_total(sweep, column)
        inverse = 1.0 / jnp.where(total > 0.0, total, 1.0)
        column = None
        for i in range(groups * CAP // row_step):
            span = slice(i * row_step, (i + 1) * row_step)
            value = weights[span, :] * inverse
            row_sum = jnp.sum(value, axis=1, keepdims=True)
            value = value * (1.0 / jnp.where(row_sum > 0.0, row_sum, 1.0))
            if sweep < SWEEPS - 1:
                weights[span, :] = value
                partial = jnp.sum(value, axis=0, keepdims=True)
                column = partial if column is None else column + partial
            else:
                assign_t[:, span] = jnp.transpose(value.astype(BF16))

    share = slots // (ny * nz)
    sizes = {"y": ny, "z": nz}
    places = {"y": (at_y, dev_y), "z": (at_z, dev_z)}
    steps, copies = {}, {}
    sem = 0
    taken_columns = [group * GROUP for group in range(width // GROUP)]
    for group in {tile[1] for tile in TILES}:
        def product(span=slice(group * GROUP, (group + 1) * GROUP)):
            value = jnp.dot(assign_t[...], rows[:, span], preferred_element_type=F32)
            part[:, :, :, span] = value.reshape(ny, nz, share, GROUP)

        steps["product", group] = product
    for index, (order, group_of, cols, long, mode, _) in enumerate(TILES):
        send1, recv1, middle, send2, recv2 = tile_bufs[5 * index:5 * index + 5]
        first = taken_columns[group_of]
        taken_columns[group_of] += cols
        window = pl.ds(first, cols)

        for stage, axis in enumerate(order):
            n = sizes[axis]
            at, dev = places[axis]
            kind = "ring" if stage == 0 else mode
            send_buf, recv_buf = (send1, recv1) if stage == 0 else (send2, recv2)
            if stage == 1:
                def chunk(k, middle=middle):
                    return middle[pl.ds(k, 1)][0]
            elif axis == "y":
                def chunk(k, window=window):
                    return part[pl.ds(k, 1), :, :, window][0]
            else:
                def chunk(k, window=window):
                    return part[:, pl.ds(k, 1), :, window][:, 0]

            messages = stage_messages(kind, n, long)
            names = [(index, stage, name, step) for name, step, _, _ in messages]
            slot_of = {name: slot for slot, name in enumerate(names)}

            def put(key, value, device, slot_of=slot_of, send_buf=send_buf, recv_buf=recv_buf, sem=sem):
                slot = slot_of[key]
                send_buf[slot] = value.astype(BF16)
                copies[key] = send(
                    send_buf.at[slot], recv_buf.at[slot], rs_send.at[sem + slot], rs_recv.at[sem + slot], device
                )

            def got(key, slot_of=slot_of, recv_buf=recv_buf):
                copies[key].wait_recv()
                return recv_buf[slot_of[key]].astype(F32)

            def total(keys, at=at, chunk=chunk, got=got, stage=stage, middle=middle, first=first, cols=cols):
                value = chunk(at(0))
                for key in keys:
                    value = value + got(key)
                if stage == 0:
                    middle[...] = value
                else:
                    final[:, first:first + cols] = value

            if kind == "ring":
                for key, (name, step, way, _) in zip(names, messages):
                    last = n // 2 if name == "far" else n // 2 - 1

                    def forward(
                        key=key, step=step, way=way, last=last, at=at, dev=dev, chunk=chunk, got=got, put=put
                    ):
                        value = chunk(at(way * (last - step + 1)))
                        if step > 1:
                            value = value + got(key[:3] + (step - 1,))
                        put(key, value, dev(way))

                    steps[key] = forward
                ends = [key for key in names if key[3] == (n // 2 if key[2] == "far" else n // 2 - 1)]
            else:
                def spread(names=names, at=at, dev=dev, chunk=chunk, put=put):
                    for key in names:
                        put(key, chunk(at(key[3])), dev(key[3]))

                steps[index, stage, "all"] = spread
                ends = names
            steps[index, stage, "sum"] = functools.partial(total, ends)
            sem += n - 1

    for key in schedule(sizes, slots):
        steps[key]()
        while len(pending) > 64:
            pending.pop(0).wait_send()

    base = cent_unit[pl.ds(pl.multiple_of(pts * share, share), share), :].astype(F32)
    out_ref[...] = unit_rms(base + 8.0 * final[...]).astype(BF16)
    for copy in pending:
        copy.wait_send()


def local(mesh_pts, mesh_own, points, parent_of, owner_of, child_count, centroids):
    ny = NY
    nz = mesh_pts // ny
    nx = mesh_own // CORES
    tokens, width = points.shape
    slots = centroids.shape[1]
    parents = owner_of.shape[0]
    share = slots // mesh_pts
    groups = mesh_own
    tile_shapes = []
    sems = 0
    for order, _, cols, _, _, _ in TILES:
        n1, n2 = (ny, nz) if order == "yz" else (nz, ny)
        tile_shapes += [
            pltpu.VMEM((n1 - 1, n2, share, cols), BF16),
            pltpu.VMEM((n1 - 1, n2, share, cols), BF16),
            pltpu.VMEM((n2, share, cols), F32),
            pltpu.VMEM((n2 - 1, share, cols), BF16),
            pltpu.VMEM((n2 - 1, share, cols), BF16),
        ]
        sems += n1 + n2 - 2
    dma = pltpu.SemaphoreType.DMA
    operands = (
        points,
        parent_of.reshape(1, groups * tokens),
        owner_of.reshape(1, parents),
        child_count.reshape(1, parents),
        centroids[0],
    )
    out = pl.pallas_call(
        functools.partial(kernel_entry, ny, nz, nx, len(tile_shapes)),
        out_shape=jax.ShapeDtypeStruct((share, width), BF16),
        in_specs=[pl.BlockSpec(memory_space=pl.ANY)] * 5,
        out_specs=pl.BlockSpec(memory_space=pltpu.VMEM),
        scratch_shapes=[
            pltpu.VMEM((1, groups * tokens), jnp.int32),
            pltpu.VMEM((1, parents), jnp.int32),
            pltpu.VMEM((1, parents), jnp.int32),
            pltpu.VMEM((tokens, width), BF16),
            pltpu.VMEM((slots, width), BF16),
            pltpu.VMEM((slots, width), BF16),
            pltpu.VMEM((tokens, width), BF16),
            pltpu.VMEM((nx * PAIR, width), BF16),
            pltpu.VMEM((groups * CAP, width), BF16),
            pltpu.VMEM((parents, slots), BF16),
            pltpu.VMEM((groups * CAP, parents), BF16),
            pltpu.VMEM((groups, tokens), F32),
            pltpu.VMEM((groups * CAP, slots), F32),
            pltpu.VMEM((slots, groups * CAP), BF16),
            pltpu.VMEM((ny, nz, share, width), F32),
            pltpu.VMEM((share, width), F32),
            pltpu.VMEM((SWEEPS, 1, slots), F32),
            pltpu.VMEM((SWEEPS, ny * nz - 1, 1, slots), F32),
            *tile_shapes,
            dma((3,)),
            dma,
            dma,
            dma((groups,)),
            dma((groups,)),
            dma((groups,)),
            dma((groups,)),
            dma((groups,)),
            dma((groups,)),
            dma((SWEEPS, ny * nz - 1)),
            dma((SWEEPS, ny * nz - 1)),
            dma((sems,)),
            dma((sems,)),
            pltpu.SemaphoreType.REGULAR((3,)),
        ],
        compiler_params=pltpu.CompilerParams(
            collective_id=0, has_side_effects=True, vmem_limit_bytes=36 * 1024 * 1024
        ),
    )(
        *(pltpu.with_memory_space_constraint(one, pltpu.HBM) for one in operands)
    )
    return out[None]


def kernel_entry(ny, nz, nx, tiles, *refs):
    head, rest = refs[:6 + 18], refs[6 + 18:]
    return kernel(ny, nz, nx, *head, rest[:tiles], *rest[tiles:])


def solution(mesh):
    in_specs = (P(("pts", "own"), None), P("pts", None), P(), P(), P("own", None, None))
    out_specs = P("own", "pts", None)
    body = functools.partial(local, mesh.shape["pts"], mesh.shape["own"])
    return jax.shard_map(body, mesh=mesh, in_specs=in_specs, out_specs=out_specs, check_vma=False)
```

```python
import functools

import jax
import jax.numpy as jnp
from jax import lax
from jax.experimental import pallas as pl
from jax.experimental.pallas import tpu as pltpu
from jax.sharding import PartitionSpec as P

SWEEPS = 2
CAP = 64
PAIR = 96
HALF = PAIR // 2
EXTRA = CAP - HALF
LAST = 512
NEVER = -1e30
CORES = 2
NY = 4
MESH = pl.DeviceIdType.MESH
F32 = jnp.float32
BF16 = jnp.bfloat16

GROUP = 256
TILES = (
    ("yz", 0, 256, -1, "direct", 0),
    ("zy", 1, 128, 1, "direct", 0),
    ("zy", 1, 128, -1, "direct", 0),
    ("zy", 2, 128, -1, "direct", 0),
    ("zy", 2, 128, 1, "direct", 0),
    ("yz", 3, 256, 1, "direct", 0),
    ("yz", 4, 128, -1, "ring", 0),
    ("yz", 4, 128, 1, "ring", 0),
    ("zy", 5, 128, -1, "direct", 0),
    ("zy", 5, 128, 1, "direct", 0),
)


def stage_messages(mode, n, long):
    far = n // 2
    if mode == "ring":
        return [("far", t, long, 1) for t in range(1, far + 1)] + [("near", t, -long, 1) for t in range(1, far)]
    return [("one", long * far, long, far)] + [
        ("one", hops * way, way, hops) for hops in range(far - 1, 0, -1) for way in (long, -long)
    ]


def tile_tasks(index, tile, sizes, slots):
    order, group, cols, long, mode, _ = tile
    share = slots
    for axis in order:
        share //= sizes[axis]
    before = ("product", group)
    tasks = {before: ((), (), 0.69, ())}
    for stage, axis in enumerate(order):
        n = sizes[axis]
        chunk = (slots // n if stage == 0 else share) * cols
        work = chunk * 1.526e-6
        kind = "ring" if stage == 0 else mode
        messages = stage_messages(kind, n, long)
        names = [(index, stage, name, step) for name, step, _, _ in messages]
        wire = [(name, axis, way, hops, chunk * 2) for name, (_, _, way, hops) in zip(names, messages)]
        done = (index, stage, "sum")
        if kind == "ring":
            for key, one in zip(names, wire):
                last = key[:3] + (key[3] - 1,)
                first = key[3] == 1
                tasks[key] = ((before,) if first else (last,), () if first else (last,), work + 0.03, (one,))
            ends = [(index, stage, "far", n // 2)] + ([(index, stage, "near", n // 2 - 1)] if n > 2 else [])
            tasks[done] = (tuple(ends), tuple(ends), 2 * work + 0.03, ())
        else:
            tasks[index, stage, "all"] = ((before,), (), n * work + 0.03, tuple(wire))
            tasks[done] = (((index, stage, "all"),), tuple(names), n * work + 0.03, ())
        before = done
    return tasks


def schedule(sizes, slots):
    rate, hop_us, next_hop_us = 46500.0, 1.5, 0.75
    tasks = {}
    for index, tile in enumerate(TILES):
        tasks.update(tile_tasks(index, tile, sizes, slots))
    sender = {message[0]: key for key, task in tasks.items() for message in task[3]}
    after = {key: [] for key in tasks}
    for key, (before, waits, _, _) in tasks.items():
        for one in before:
            after[one].append((key, 0.0))
        for one in waits:
            after[sender[one]].append((key, hop_us))
    chain = {}

    def length(key):
        if key not in chain:
            chain[key] = tasks[key][2] + max([gap + length(one) for one, gap in after[key]], default=0.0)
        return chain[key]

    def rank(key):
        heads = [one[0] for one, _ in after[key]] if key[0] == "product" else [key[0]]
        return length(key) + max(TILES[index][5] for index in heads)

    now, order, arrival, link_free, done = 0.0, [], {}, {}, set()
    while len(order) < len(tasks):
        ready = []
        for key, (before, waits, _, _) in tasks.items():
            if key not in done and all(one in done for one in before) and all(one in arrival for one in waits):
                ready.append((max([arrival[one] for one in waits], default=0.0), key))
        started = [one for one in ready if one[0] <= now]
        if started:
            at, key = max(started, key=lambda one: rank(one[1]))
        else:
            at, key = min(ready, key=lambda one: (one[0], -rank(one[1])))
        now = max(now, at) + tasks[key][2]
        for name, axis, way, hops, size in tasks[key][3]:
            start = max(now, link_free.get((axis, way), 0.0))
            link_free[axis, way] = start + hops * size / rate
            arrival[name] = link_free[axis, way] + hop_us + next_hop_us * (hops - 1)
        done.add(key)
        order.append(key)
    return order


def unit_rms(values):
    values = values.astype(F32)
    return values * lax.rsqrt(jnp.mean(values * values, axis=-1, keepdims=True) + 1e-06)


def iota(shape, dim):
    return lax.broadcasted_iota(jnp.int32, shape, dim).astype(F32)


def kernel(
    ny, nz, nx,
    points_hbm, parent_hbm, owner_hbm, count_hbm, cent_hbm, out_ref,
    parent_ref, owner_ref, count_ref, point_raw, cent_raw, cent_unit, point_unit, packed, rows, member, onehot, place, weights, assign_t, part, final,
    sum_send, sum_recv, tile_bufs,
    small_sem, point_sem, cent_sem, x_send, x_recv, l_send, l_recv, f_send, f_recv, s_send, s_recv, rs_send, rs_recv,
    round_sem,
):
    pts, me = lax.axis_index("pts"), lax.axis_index("own")
    y, z = lax.div(pts, nz), lax.rem(pts, nz)
    x, core = lax.div(me, CORES), lax.rem(me, CORES)
    groups = nx * CORES
    tokens, width = points_hbm.shape
    parents = owner_hbm.shape[1]
    slots = cent_hbm.shape[0]

    def own_at(dx, dc, sign):
        other = lax.rem(x + (dx if sign > 0 else nx - dx), nx)
        return other * CORES + (core if dc == 0 else 1 - core)

    def at_y(step):
        return lax.rem(y + step + ny, ny)

    def at_z(step):
        return lax.rem(z + step + nz, nz)

    def dev_y(step):
        return (at_y(step) * nz + z, me)

    def dev_z(step):
        return (y * nz + at_z(step), me)

    offsets = [(dx, dc) for dx in range(nx) for dc in range(CORES)]
    barrier = pltpu.get_barrier_semaphore()
    peers = [(pts, own_at(dx, dc, 1)) for dx, dc in offsets if (dx, dc) != (0, 0)]
    peers += [dev_y(s) for s in range(1, ny)] + [dev_z(1), dev_z(-1)]
    for peer in peers:
        pl.semaphore_signal(barrier, inc=1, device_id=peer, device_id_type=MESH)
    small = [
        pltpu.make_async_copy(source, target, small_sem.at[i])
        for i, (source, target) in enumerate(
            ((owner_hbm, owner_ref), (count_hbm, count_ref), (parent_hbm, parent_ref))
        )
    ]
    for copy in small:
        copy.start()
    point_copy = pltpu.make_async_copy(points_hbm, point_raw, point_sem)
    point_copy.start()
    cent_copy = pltpu.make_async_copy(cent_hbm, cent_raw, cent_sem)
    cent_copy.start()

    pending = []

    def send(src, dst, send_sem, recv_sem, device):
        copy = pltpu.make_async_remote_copy(
            src_ref=src, dst_ref=dst, send_sem=send_sem, recv_sem=recv_sem,
            device_id=device, device_id_type=MESH,
        )
        copy.start()
        pending.append(copy)
        return copy

    for copy in small:
        copy.wait()

    square = (parents, parents)
    owner_row = owner_ref[...].astype(F32)
    count_row = count_ref[...].astype(F32)
    diagonal = iota(square, 0) == iota(square, 1)
    owner_col = jnp.sum(jnp.where(diagonal, owner_row, 0.0), axis=1, keepdims=True)
    count_col = jnp.sum(jnp.where(diagonal, count_row, 0.0), axis=1, keepdims=True)
    upper = jnp.where(iota((tokens, tokens), 0) <= iota((tokens, tokens), 1), 1.0, 0.0).astype(BF16)
    parent_iota = iota((parents, tokens), 0)

    def owners_of_block(index):
        parent = parent_ref[:, pl.ds(pl.multiple_of(index * tokens, tokens), tokens)].astype(F32)
        return parent, jnp.sum(jnp.where(parent_iota == parent, owner_col, 0.0), axis=0, keepdims=True)

    _, my_owner = owners_of_block(me)
    goes = my_owner == iota((groups, tokens), 0)
    rank = jnp.dot(jnp.where(goes, 1.0, 0.0).astype(BF16), upper, preferred_element_type=F32)
    odd = lax.rem(lax.broadcasted_iota(jnp.int32, (groups, tokens), 0), CORES) == 1
    place[...] = jnp.where(goes, jnp.where(odd, PAIR - rank, rank - 1.0), -1.0)
    point_copy.wait()
    point_unit[...] = unit_rms(point_raw[...]).astype(BF16)

    pair_iota = iota((PAIR, tokens), 0)
    near, far = (1, nx - 1), (nx // 2,)
    blocks = [(dx, dc) for dx in (0,) + far + near for dc in range(CORES)]
    block_of = {offset: i for i, offset in enumerate(blocks)}

    def pack(group):
        picks = []
        for dx in group:
            chip = lax.rem(x + dx, nx) * CORES
            taken = place[pl.ds(chip, 1), :] == pair_iota
            for other in range(1, CORES):
                taken = taken | (place[pl.ds(chip + other, 1), :] == pair_iota)
            picks.append(jnp.where(taken, 1.0, 0.0).astype(BF16))
        block = jnp.dot(jnp.concatenate(picks, axis=0), point_unit[...], preferred_element_type=F32).astype(BF16)
        for i, dx in enumerate(group):
            packed[dx * PAIR:(dx + 1) * PAIR, :] = block[i * PAIR:(i + 1) * PAIR]

    def part_of(start, size):
        return pl.ds(pl.multiple_of(start, EXTRA), size)

    arrivals, lasts, forwards = {}, {}, {}

    early, late = slice(0, width - LAST), slice(width - LAST, width)

    def depart(group):
        for window in (early, late):
            for dx in group:
                for dc in range(CORES):
                    k = block_of[dx, dc]
                    to_core = core if dc == 0 else 1 - core
                    device = (pts, own_at(dx, dc, 1))
                    span = slice(0, width) if group is far else window
                    if window is early:
                        arrivals[dx, dc] = send(
                            packed.at[part_of(dx * PAIR + HALF * to_core, HALF), span],
                            rows.at[part_of(k * CAP + EXTRA * to_core, HALF), span],
                            x_send.at[k], x_recv.at[k], device,
                        )
                    elif group is near:
                        lasts[dx, dc] = send(
                            packed.at[part_of(dx * PAIR + (PAIR - CAP) * to_core, CAP), span],
                            rows.at[pl.ds(k * CAP, CAP), span],
                            l_send.at[k], l_recv.at[k], device,
                        )

    def hand_over(group, span):
        for dx in group:
            for dc in range(CORES):
                k, other = block_of[dx, dc], block_of[dx, 1 - dc]
                arrivals[dx, dc].wait_recv()
                forwards[dx, dc] = send(
                    rows.at[part_of(k * CAP + 2 * EXTRA - EXTRA * core, EXTRA), span],
                    rows.at[part_of(other * CAP + HALF * core, EXTRA), span],
                    f_send.at[k], f_recv.at[other], (pts, own_at(0, 1, 1)),
                )

    def handed_over(group):
        for dx in group:
            for dc in range(CORES):
                forwards[dx, dc].wait_recv()

    pack(far)
    pl.semaphore_wait(barrier, len(peers))
    for step in (1, -1):
        pl.semaphore_signal(round_sem.at[0], inc=1, device_id=dev_z(step), device_id_type=MESH)
    depart(far)
    pack(near)
    depart(near)
    pack((0,))
    mine, theirs = block_of[0, 0], block_of[0, 1]
    rows[mine * CAP:(mine + 1) * CAP, :] = packed[part_of((PAIR - CAP) * core, CAP), :]
    arrivals[0, 1] = send(
        packed.at[part_of((PAIR - CAP) * (1 - core), CAP)], rows.at[pl.ds(theirs * CAP, CAP)],
        x_send.at[theirs], x_recv.at[theirs], (pts, own_at(0, 1, 1)),
    )

    first_col = jnp.sum(
        jnp.where((owner_col == owner_row) & (iota(square, 1) < iota(square, 0)), count_row, 0.0),
        axis=1, keepdims=True,
    )
    my_index = me.astype(F32)
    slot_row = iota((parents, slots), 1)
    member[...] = jnp.where(
        (owner_col == my_index) & (slot_row >= first_col) & (slot_row < first_col + count_col), 1.0, 0.0
    ).astype(BF16)
    block_parent, block_live = [], []
    for dx, dc in blocks:
        parent, owner = owners_of_block(own_at(dx, dc, -1))
        block_parent.append(parent)
        block_live.append(owner == my_index)
    live = jnp.concatenate([jnp.where(one, 1.0, 0.0) for one in block_live], axis=0)
    rank = jnp.dot(live.astype(BF16), upper, preferred_element_type=F32)
    spot = jnp.where(live > 0.5, rank - 1.0, -1.0)
    slot_iota = iota((CAP, tokens), 0)
    slot_iota = jnp.where(core == 0, slot_iota, (CAP - 1.0) - slot_iota)
    for k in range(groups):
        chosen = spot[k:k + 1, :] == slot_iota
        parent = jnp.sum(jnp.where(chosen, block_parent[k] + 1.0, 0.0), axis=1, keepdims=True) - 1.0
        onehot[k * CAP:(k + 1) * CAP, :] = jnp.where(parent == iota((CAP, parents), 1), 1.0, 0.0).astype(BF16)

    cent_copy.wait()
    step_rows = 64

    @pl.loop(0, slots // step_rows)
    def _(i):
        span = pl.ds(pl.multiple_of(i * step_rows, step_rows), step_rows)
        cent_unit[span, :] = unit_rms(cent_raw[span, :]).astype(BF16)

    pl.semaphore_wait(round_sem.at[0], 2)
    for step in (2, -2):
        pl.semaphore_signal(round_sem.at[1], inc=1, device_id=dev_z(step), device_id_type=MESH)

    scale = 1.0 / (width * 0.05)
    wide = 256

    def score(span, cols, depth):
        return lax.dot_general(
            rows[span, depth], cent_unit[cols, depth], (((1,), (1,)), ((), ())), preferred_element_type=F32
        )

    def allowed(span, cols):
        return jnp.dot(onehot[span, :], member[:, cols], preferred_element_type=F32) > 0.5

    def weigh(span, cols, value):
        weights[span, cols] = value
        return jnp.sum(value, axis=0, keepdims=True)

    first_rows = (1 + len(far)) * CORES * CAP
    top, bottom = slice(0, first_rows), slice(first_rows, groups * CAP)
    slot_cols = [slice(n * wide, (n + 1) * wide) for n in range(slots // wide)]
    for cols in slot_cols:
        weights[bottom, cols] = jnp.where(allowed(bottom, cols), 0.0, NEVER)
    arrivals[0, 1].wait_recv()
    hand_over(far, slice(0, width))
    handed_over(far)
    sums = [
        weigh(top, cols, jnp.where(allowed(top, cols), jnp.exp(score(top, cols, slice(0, width)) * scale), 0.0))
        for cols in slot_cols
    ]
    pl.semaphore_wait(round_sem.at[1], 2)
    for step in (1, -1):
        pl.semaphore_signal(round_sem.at[2], inc=1, device_id=dev_z(step), device_id_type=MESH)
    hand_over(near, early)
    handed_over(near)
    for cols in slot_cols:
        weights[bottom, cols] += score(bottom, cols, early)
    for dx in near:
        for dc in range(CORES):
            lasts[dx, dc].wait_recv()
    for n, cols in enumerate(slot_cols):
        value = jnp.exp((weights[bottom, cols] + score(bottom, cols, late)) * scale)
        sums[n] = sums[n] + weigh(bottom, cols, value)
    column = jnp.concatenate(sums, axis=1)
    pl.semaphore_wait(round_sem.at[2], 2)

    plane = sorted(
        ((dy, dz) for dy in range(ny) for dz in range(nz) if (dy, dz) != (0, 0)),
        key=lambda one: -min(one[0], ny - one[0]) - min(one[1], nz - one[1]),
    )

    def column_total(sweep, local):
        sum_send[sweep] = local
        copies = [
            send(sum_send.at[sweep], sum_recv.at[sweep, k], s_send.at[sweep, k], s_recv.at[sweep, k],
                 (at_y(dy) * nz + at_z(dz), me))
            for k, (dy, dz) in enumerate(plane)
        ]
        total = local
        for k, copy in reversed(list(enumerate(copies))):
            copy.wait_recv()
            total = total + sum_recv[sweep, k]
        return total

    row_step = 128
    for sweep in range(SWEEPS):
        total = column_total(sweep, column)
        inverse = 1.0 / jnp.where(total > 0.0, total, 1.0)
        column = None
        for i in range(groups * CAP // row_step):
            span = slice(i * row_step, (i + 1) * row_step)
            value = weights[span, :] * inverse
            row_sum = jnp.sum(value, axis=1, keepdims=True)
            value = value * (1.0 / jnp.where(row_sum > 0.0, row_sum, 1.0))
            if sweep < SWEEPS - 1:
                weights[span, :] = value
                partial = jnp.sum(value, axis=0, keepdims=True)
                column = partial if column is None else column + partial
            else:
                assign_t[:, span] = jnp.transpose(value.astype(BF16))

    share = slots // (ny * nz)
    sizes = {"y": ny, "z": nz}
    places = {"y": (at_y, dev_y), "z": (at_z, dev_z)}
    steps, copies = {}, {}
    sem = 0
    taken_columns = [group * GROUP for group in range(width // GROUP)]
    for group in {tile[1] for tile in TILES}:
        def product(span=slice(group * GROUP, (group + 1) * GROUP)):
            value = jnp.dot(assign_t[...], rows[:, span], preferred_element_type=F32)
            part[:, :, :, span] = value.reshape(ny, nz, share, GROUP)

        steps["product", group] = product
    for index, (order, group_of, cols, long, mode, _) in enumerate(TILES):
        send1, recv1, middle, send2, recv2 = tile_bufs[5 * index:5 * index + 5]
        first = taken_columns[group_of]
        taken_columns[group_of] += cols
        window = pl.ds(first, cols)

        for stage, axis in enumerate(order):
            n = sizes[axis]
            at, dev = places[axis]
            kind = "ring" if stage == 0 else mode
            send_buf, recv_buf = (send1, recv1) if stage == 0 else (send2, recv2)
            if stage == 1:
                def chunk(k, middle=middle):
                    return middle[pl.ds(k, 1)][0]
            elif axis == "y":
                def chunk(k, window=window):
                    return part[pl.ds(k, 1), :, :, window][0]
            else:
                def chunk(k, window=window):
                    return part[:, pl.ds(k, 1), :, window][:, 0]

            messages = stage_messages(kind, n, long)
            names = [(index, stage, name, step) for name, step, _, _ in messages]
            slot_of = {name: slot for slot, name in enumerate(names)}

            def put(key, value, device, slot_of=slot_of, send_buf=send_buf, recv_buf=recv_buf, sem=sem):
                slot = slot_of[key]
                send_buf[slot] = value.astype(BF16)
                copies[key] = send(
                    send_buf.at[slot], recv_buf.at[slot], rs_send.at[sem + slot], rs_recv.at[sem + slot], device
                )

            def got(key, slot_of=slot_of, recv_buf=recv_buf):
                copies[key].wait_recv()
                return recv_buf[slot_of[key]].astype(F32)

            def total(keys, at=at, chunk=chunk, got=got, stage=stage, middle=middle, first=first, cols=cols):
                value = chunk(at(0))
                for key in keys:
                    value = value + got(key)
                if stage == 0:
                    middle[...] = value
                else:
                    final[:, first:first + cols] = value

            if kind == "ring":
                for key, (name, step, way, _) in zip(names, messages):
                    last = n // 2 if name == "far" else n // 2 - 1

                    def forward(
                        key=key, step=step, way=way, last=last, at=at, dev=dev, chunk=chunk, got=got, put=put
                    ):
                        value = chunk(at(way * (last - step + 1)))
                        if step > 1:
                            value = value + got(key[:3] + (step - 1,))
                        put(key, value, dev(way))

                    steps[key] = forward
                ends = [key for key in names if key[3] == (n // 2 if key[2] == "far" else n // 2 - 1)]
            else:
                def spread(names=names, at=at, dev=dev, chunk=chunk, put=put):
                    for key in names:
                        put(key, chunk(at(key[3])), dev(key[3]))

                steps[index, stage, "all"] = spread
                ends = names
            steps[index, stage, "sum"] = functools.partial(total, ends)
            sem += n - 1

    for key in schedule(sizes, slots):
        steps[key]()
        while len(pending) > 64:
            pending.pop(0).wait_send()

    base = cent_unit[pl.ds(pl.multiple_of(pts * share, share), share), :].astype(F32)
    out_ref[...] = unit_rms(base + 8.0 * final[...]).astype(BF16)
    for copy in pending:
        copy.wait_send()


def local(mesh_pts, mesh_own, points, parent_of, owner_of, child_count, centroids):
    ny = NY
    nz = mesh_pts // ny
    nx = mesh_own // CORES
    tokens, width = points.shape
    slots = centroids.shape[1]
    parents = owner_of.shape[0]
    share = slots // mesh_pts
    groups = mesh_own
    tile_shapes = []
    sems = 0
    for order, _, cols, _, _, _ in TILES:
        n1, n2 = (ny, nz) if order == "yz" else (nz, ny)
        tile_shapes += [
            pltpu.VMEM((n1 - 1, n2, share, cols), BF16),
            pltpu.VMEM((n1 - 1, n2, share, cols), BF16),
            pltpu.VMEM((n2, share, cols), F32),
            pltpu.VMEM((n2 - 1, share, cols), BF16),
            pltpu.VMEM((n2 - 1, share, cols), BF16),
        ]
        sems += n1 + n2 - 2
    dma = pltpu.SemaphoreType.DMA
    operands = (
        points,
        parent_of.reshape(1, groups * tokens),
        owner_of.reshape(1, parents),
        child_count.reshape(1, parents),
        centroids[0],
    )
    out = pl.pallas_call(
        functools.partial(kernel_entry, ny, nz, nx, len(tile_shapes)),
        out_shape=jax.ShapeDtypeStruct((share, width), BF16),
        in_specs=[pl.BlockSpec(memory_space=pl.ANY)] * 5,
        out_specs=pl.BlockSpec(memory_space=pltpu.VMEM),
        scratch_shapes=[
            pltpu.VMEM((1, groups * tokens), jnp.int32),
            pltpu.VMEM((1, parents), jnp.int32),
            pltpu.VMEM((1, parents), jnp.int32),
            pltpu.VMEM((tokens, width), BF16),
            pltpu.VMEM((slots, width), BF16),
            pltpu.VMEM((slots, width), BF16),
            pltpu.VMEM((tokens, width), BF16),
            pltpu.VMEM((nx * PAIR, width), BF16),
            pltpu.VMEM((groups * CAP, width), BF16),
            pltpu.VMEM((parents, slots), BF16),
            pltpu.VMEM((groups * CAP, parents), BF16),
            pltpu.VMEM((groups, tokens), F32),
            pltpu.VMEM((groups * CAP, slots), F32),
            pltpu.VMEM((slots, groups * CAP), BF16),
            pltpu.VMEM((ny, nz, share, width), F32),
            pltpu.VMEM((share, width), F32),
            pltpu.VMEM((SWEEPS, 1, slots), F32),
            pltpu.VMEM((SWEEPS, ny * nz - 1, 1, slots), F32),
            *tile_shapes,
            dma((3,)),
            dma,
            dma,
            dma((groups,)),
            dma((groups,)),
            dma((groups,)),
            dma((groups,)),
            dma((groups,)),
            dma((groups,)),
            dma((SWEEPS, ny * nz - 1)),
            dma((SWEEPS, ny * nz - 1)),
            dma((sems,)),
            dma((sems,)),
            pltpu.SemaphoreType.REGULAR((3,)),
        ],
        compiler_params=pltpu.CompilerParams(
            collective_id=0, has_side_effects=True, vmem_limit_bytes=36 * 1024 * 1024
        ),
    )(
        *(pltpu.with_memory_space_constraint(one, pltpu.HBM) for one in operands)
    )
    return out[None]


def kernel_entry(ny, nz, nx, tiles, *refs):
    head, rest = refs[:6 + 18], refs[6 + 18:]
    return kernel(ny, nz, nx, *head, rest[:tiles], *rest[tiles:])


def solution(mesh):
    in_specs = (P(("pts", "own"), None), P("pts", None), P(), P(), P("own", None, None))
    out_specs = P("own", "pts", None)
    body = functools.partial(local, mesh.shape["pts"], mesh.shape["own"])
    return jax.shard_map(body, mesh=mesh, in_specs=in_specs, out_specs=out_specs, check_vma=False)
```
